32 devices in a mesh: group: 2 (over y), sky: 4 (over z), exp: 2 (over x), band: 2 (over core).
Axes of the slice: x: 2, y: 2, z: 4, core: 2. Of those that a mesh axis runs over, the one named last changes fastest.
Arguments:
- sky: bfloat16 [6, 512, 2048], P('band', None, ('group', 'sky')), parts along dimension 2, may hold values from -6 to 6
- observed: bfloat16 [6, 16, 64, 64], P('band', ('group', 'sky', 'exp')), parts along dimension 1, may hold values from -4 to 4
- psf: bfloat16 [6, 16, 625], P('band', ('group', 'sky', 'exp')), parts along dimension 1, may hold values from 0.0039978027 to 0.039794922
- anchor: int32 [6, 16], P('band', 'group'), parts along dimension 1, may hold values from 0 to 2, as said below
- offsets: int32 [6, 2, 16], P('band', None, 'group'), parts along dimension 2, may hold values from 0 to 424
Outputs:
- gradient: float32 [6, 512, 2048], P('band', None, ('group', 'sky')), parts along dimension 2
The draws below stay inside these ranges and needn't reach their ends.
There are 2 independent parts, one for each index of `group`. The reference program is written for one: setup_inputs(seed, part) draws one part's arguments, and reference() takes and returns one part's arrays. A program takes and returns all parts, laid end to end along the dimension named above; each array names one. Nothing has to cross between parts.
Inputs may be any that keep to these rules, and one draw needn't show every extreme that they name: Each exposure's window lies within tile columns a and a + 1 and within the two tile rows. Within each band, the 1 exposures of one device (aligned blocks of 1) have distinct even anchor columns.
All inputs are finite; a program needn't handle non-finite values.
Results may differ from the reference program's by a relative error of at most 0.0028.
Values may be sent and summed in bfloat16 or wider, within the bound.
No kernel may reach another device: no remote copies, remote signals or barrier semaphores. Data moves between devices by JAX's collectives and lax.ppermute only.
A program may use at most 64 MiB of HBM per device.

```python
import math
import jax
import jax.numpy as jnp
from jax import lax

BANDS = 6
TILE = 256
PSF = 25
STAMP = 64
WIN = 88
EXP_DEV = 1
EXPOSURES = 8
SKY_ROWS = 512
SKY_COLS = 1024
N_SKY = 4


def draw_anchor(key, part):
    device_rows = BANDS * (EXPOSURES // EXP_DEV)
    keys = jax.random.split(key, device_rows)

    def pick_columns(one_key):
        return jax.random.permutation(one_key, N_SKY // 2)[:EXP_DEV]
    picks = jax.vmap(pick_columns)(keys)
    return (2 * picks).reshape(BANDS, EXPOSURES).astype(jnp.int32)


def with_ends(entries, own_key, smallest, top_value):
    spot = [jax.random.randint(jax.random.fold_in(own_key, axis), (), 0, length) for axis, length in enumerate(entries.shape)]
    main_axis = entries.shape.index(max(entries.shape))
    beside = spot[:main_axis] + [(spot[main_axis] + 1) % entries.shape[main_axis]] + spot[main_axis + 1:]
    return entries.at[tuple(spot)].set(smallest).at[tuple(beside)].set(top_value)


def block_levels(stream_key, shape, pieces, least, largest):
    def one(axis_at, parts):
        steps = jax.random.uniform(jax.random.fold_in(jax.random.fold_in(stream_key, 6), axis_at), (parts,), jnp.float32, least / len(pieces), largest / len(pieces))
        return jnp.repeat(jnp.exp(steps), shape[axis_at] // parts).reshape((-1,) + (1,) * (len(shape) - axis_at - 1))

    level = one(*pieces[0])
    for cut in pieces[1:]:
        level = level * one(*cut)
    return level


def noise(key, dims, spread, reach, cuts=(), kind=jnp.bfloat16):
    drawn = jax.random.normal(key, dims, jnp.float32) * spread
    if len(cuts) > 0:
        drawn = block_levels(key, dims, cuts, -0.22, 0.18) * drawn
    return jnp.clip(drawn, min=-reach, max=reach).astype(kind)


def setup_inputs(seed: int = 0, part: int = 0) -> dict:
    arg_keys = jax.random.split(jax.random.key(seed), 6)
    part_keys = jax.random.split(jax.random.fold_in(arg_keys[5], part), 6)
    sky = noise(part_keys[0], (BANDS, SKY_ROWS, SKY_COLS), 1.0, 6.0, ((0, 2), (2, 4)))
    observed = noise(part_keys[1], (BANDS, EXPOSURES, STAMP, STAMP), 0.5, 4.0, ((0, 2), (1, 8)))
    psf = jnp.clip(jnp.exp(math.log(0.039794922) - 2.2979944 * jax.random.uniform(part_keys[2], (BANDS, EXPOSURES, PSF * PSF), jnp.float32) ** block_levels(part_keys[2], (BANDS, EXPOSURES, PSF * PSF), ((0, 2), (1, 8)), -0.2, 0.2)), 0.0039978027, 0.039794922).astype(jnp.bfloat16)
    anchor = draw_anchor(jax.random.fold_in(jax.random.fold_in(arg_keys[5], part), 71), part)
    offsets = with_ends(jax.random.randint(part_keys[4], (BANDS, 2, EXPOSURES), 0, 2 * TILE - WIN + 1), jax.random.fold_in(part_keys[4], 1), 0, 2 * TILE - WIN).astype(jnp.int32)
    return {"sky": sky, "observed": observed, "psf": psf, "anchor": anchor, "offsets": offsets}


def place_window(total, item):
    update, row_start, col_start = item
    current = lax.dynamic_slice(total, (row_start, col_start), (WIN, WIN))
    return lax.dynamic_update_slice(total, current + update, (row_start, col_start)), None


def band_gradient(sky_band, observed_band, psf_band, anchor_band, offset_band):
    kernels = psf_band.astype(jnp.float32).reshape(EXPOSURES, 1, PSF, PSF)
    row_start = offset_band[0].astype(jnp.int32)
    col_start = (anchor_band * TILE + offset_band[1]).astype(jnp.int32)

    def cut_window(row_pos, col_pos):
        return lax.dynamic_slice(sky_band, (row_pos, col_pos), (WIN, WIN))

    windows = jax.vmap(cut_window)(row_start, col_start).astype(jnp.float32)
    model = lax.conv_general_dilated(windows[None], kernels, (1, 1), "VALID", feature_group_count=EXPOSURES, precision=lax.Precision.HIGHEST)[0]
    residual = (model - observed_band.astype(jnp.float32)).astype(jnp.bfloat16)
    residual = lax.optimization_barrier(residual).astype(jnp.float32)
    padded = jnp.pad(residual, ((0, 0), (PSF - 1, PSF - 1), (PSF - 1, PSF - 1)))
    flipped = kernels[:, :, ::-1, ::-1]
    backs = lax.conv_general_dilated(padded[None], flipped, (1, 1), "VALID", feature_group_count=EXPOSURES, precision=lax.Precision.HIGHEST)[0]
    backs = lax.optimization_barrier(backs.astype(jnp.bfloat16)).astype(jnp.float32)
    total, unused = lax.scan(place_window, jnp.zeros((SKY_ROWS, SKY_COLS), jnp.float32), (backs, row_start, col_start))
    return total


def reference(sky, observed, psf, anchor, offsets):
    results = []
    for band_pos in range(BANDS):
        results.append(band_gradient(sky[band_pos], observed[band_pos], psf[band_pos], anchor[band_pos], offsets[band_pos]))
    return jnp.stack(results, axis=0)
```

```python
import functools

import jax
import jax.numpy as jnp
from jax import lax
from jax.experimental import pallas as pl
from jax.experimental.pallas import tpu as pltpu
from jax.sharding import PartitionSpec as P

TILE = 256
PSF = 25
STAMP = 64
WIN = 88
LANES = 128
PAIRS = (PSF + 1) // 2
ROWS = 48
WPAD = 96
OWN = TILE // LANES
STRIP = OWN + 1


def lane_of(shape):
    return lax.broadcasted_iota(jnp.int32, shape, 1)


def row_of(shape):
    return lax.broadcasted_iota(jnp.int32, shape, 0)


def pack_kernel(spread_ref, obs_ref, psf_ref, out_ref):
    half = STAMP // 2
    taps = psf_ref.shape[-1]
    for i in range(obs_ref.shape[0]):
        obs = obs_ref[i].astype(jnp.float32)
        both = jnp.concatenate([obs[:half], obs[half:]], axis=1)
        out_ref[i, 0:half, :] = both.astype(jnp.bfloat16)
        flat = jnp.broadcast_to(psf_ref[i : i + 1, :].astype(jnp.float32), (16, taps))
        gap = lane_of((16, taps)) - 2 * PSF * row_of((16, taps))
        mine = jnp.where((gap >= 0) & (gap < 2 * PSF), flat, 0.0).astype(jnp.bfloat16)
        rows = jnp.dot(mine, spread_ref[...], preferred_element_type=jnp.float32)
        out_ref[i, half:ROWS, :] = rows.astype(jnp.bfloat16)


def pack(observed, psf):
    bands, per_device = observed.shape[:2]
    count = bands * per_device
    taps = psf.shape[-1]
    k = jnp.arange(taps, dtype=jnp.int32)[:, None] % (2 * PSF)
    place = jnp.where(k < PSF, -k % LANES, STAMP - (k - PSF))
    spread = (place == jnp.arange(LANES, dtype=jnp.int32)[None, :]).astype(jnp.bfloat16)
    vmem = pl.BlockSpec(memory_space=pltpu.VMEM)
    out = pl.pallas_call(
        pack_kernel,
        out_shape=jax.ShapeDtypeStruct((count, ROWS, LANES), jnp.bfloat16),
        in_specs=[vmem] * 3,
        out_specs=vmem,
        name="pack",
    )(spread, observed.reshape(count, STAMP, STAMP), psf.reshape(count, taps))
    return out.reshape(bands, per_device, ROWS, LANES)


def work_kernel(layout, bands, slots, rows_total, row_ref, col_ref, me_ref, sky_ref, halo_ref, *rest):
    pieces = rest[: len(layout)]
    out_ref, strip, total, blocks, banded, wide, rows_a, rows_r, sems, out_sems = rest[len(layout) :]
    position = me_ref[0]
    parity = me_ref[1]
    copies = []
    for at, (mask, piece) in enumerate(zip(layout, pieces)):
        if mask is None:
            dst = blocks
        else:
            dst = blocks.at[pl.ds(jnp.bitwise_xor(position, mask), 1)]
        copies.append(pltpu.make_async_copy(piece, dst, sems.at[at]))
    for copy in copies:
        copy.start()

    for b in range(bands):
        for t in range(OWN):
            strip[b, parity + t, 0:rows_total, :] = sky_ref[b, :, t * LANES : (t + 1) * LANES].astype(jnp.float32)
        strip[b, OWN * (1 - parity), 0:rows_total, :] = halo_ref[b].astype(jnp.float32)
        for t in range(STRIP):
            strip[b, t, rows_total : rows_total + 8, :] = jnp.zeros((8, LANES), jnp.float32)
            total[b, t] = jnp.zeros((rows_total, LANES), jnp.float32)
    rows_r[...] = jnp.zeros(rows_r.shape, jnp.float32)
    for copy in copies:
        copy.wait()

    lane_w = lane_of((WPAD, LANES))
    gap = row_of((WPAD, LANES)) - lane_w % STAMP
    inside = (gap >= 0) & (gap < PSF) & (row_of((WPAD, LANES)) < WIN)
    half = STAMP // 2

    def visit(index, carry):
        b = index // slots
        n = index - b * slots
        start = col_ref[b, n]

        @pl.when(start >= 0)
        def _():
            top = row_ref[b, n]
            tile = start // LANES
            shift = start - tile * LANES
            nxt = jnp.minimum(tile + 1, STRIP - 1)
            back_shift = (LANES - shift) % LANES
            left = pltpu.roll(strip[b, tile, pl.ds(top, WPAD), :], back_shift, 1)
            right = pltpu.roll(strip[b, nxt, pl.ds(top, WPAD), :], back_shift, 1)
            window = jnp.where(lane_w < LANES - shift, left, right).astype(jnp.bfloat16)
            taps = blocks[n, b, half:ROWS, :].astype(jnp.float32)
            for m in range(PAIRS):
                spread = jnp.broadcast_to(taps[m : m + 1, :], (WPAD, LANES))
                turned = pltpu.roll(spread, 0, 1, stride=1, stride_axis=0)
                banded[:, m * LANES : (m + 1) * LANES] = jnp.where(inside, turned, 0.0).astype(jnp.bfloat16)
            for m in range(PAIRS):
                wide[m] = jnp.dot(
                    window[:, :WPAD],
                    banded[:, m * LANES : (m + 1) * LANES],
                    preferred_element_type=jnp.float32,
                )
            acc = wide[0, 0:72, :]
            for m in range(1, PAIRS):
                acc = acc + wide[m, 2 * m : 2 * m + 72, :]
            rows_a[...] = acc
            model = rows_a[0:STAMP, :] + pltpu.roll(rows_a[1 : STAMP + 1, :], STAMP, 1)
            obs = blocks[n, b, 0:half, :].astype(jnp.float32)
            obs = jnp.concatenate([obs, pltpu.roll(obs, STAMP, 1)], axis=0)
            residual = (model - obs).astype(jnp.bfloat16).astype(jnp.float32)
            low = lane_of((STAMP, LANES)) < STAMP
            residual = jnp.where(low, residual, 0.0)
            rows_r[PSF - 1 : PSF - 1 + STAMP, :] = residual
            rows_r[PSF - 1 + STAMP : PSF - 1 + 72, :] = jnp.zeros((8, LANES), jnp.float32)
            upper = pltpu.roll(rows_r[PSF - 2 : PSF - 2 + 72, :], STAMP, 1)
            rows_r[PSF - 1 : PSF - 1 + 72, :] = rows_r[PSF - 1 : PSF - 1 + 72, :] + upper
            back = None
            for m in range(PAIRS):
                lhs = rows_r[PSF - 1 - 2 * m : PSF - 1 - 2 * m + WIN, :].astype(jnp.bfloat16)
                term = lax.dot_general(
                    lhs,
                    banded[:, m * LANES : (m + 1) * LANES],
                    (((1,), (1,)), ((), ())),
                    preferred_element_type=jnp.float32,
                )
                back = term if back is None else back + term
            back = back.astype(jnp.bfloat16).astype(jnp.float32)
            back = jnp.concatenate([back, jnp.zeros((WIN, LANES - WPAD), jnp.float32)], axis=1)
            back = pltpu.roll(back, shift, 1)
            lane_b = lane_of((WIN, LANES))
            total[b, tile, pl.ds(top, WIN), :] += jnp.where(lane_b >= shift, back, 0.0)
            total[b, nxt, pl.ds(top, WIN), :] += jnp.where(lane_b < shift, back, 0.0)

        return carry

    lax.fori_loop(0, bands * slots, visit, 0)
    outs = []
    for b in range(bands):
        for t in range(OWN):
            outs.append(
                pltpu.make_async_copy(
                    total.at[b, parity + t],
                    out_ref.at[b, :, pl.ds(t * LANES, LANES)],
                    out_sems.at[b, t],
                )
            )
    for copy in outs:
        copy.start()
    for copy in outs:
        copy.wait()


def work(rows, cols, me, sky, halo, pieces, layout, slots):
    bands, rows_total = sky.shape[:2]
    smem = pl.BlockSpec(memory_space=pltpu.SMEM)
    vmem = pl.BlockSpec(memory_space=pltpu.VMEM)
    anywhere = pl.BlockSpec(memory_space=pl.ANY)
    return pl.pallas_call(
        functools.partial(work_kernel, layout, bands, slots, rows_total),
        out_shape=jax.ShapeDtypeStruct((bands, rows_total, TILE), jnp.float32),
        in_specs=[smem, smem, smem, vmem, vmem] + [anywhere] * len(pieces),
        out_specs=anywhere,
        scratch_shapes=[
            pltpu.VMEM((bands, STRIP, rows_total + 8, LANES), jnp.float32),
            pltpu.VMEM((bands, STRIP, rows_total, LANES), jnp.float32),
            pltpu.VMEM((slots, bands, ROWS, LANES), jnp.bfloat16),
            pltpu.VMEM((WPAD, PAIRS * LANES), jnp.bfloat16),
            pltpu.VMEM((PAIRS, WPAD, LANES), jnp.float32),
            pltpu.VMEM((72, LANES), jnp.float32),
            pltpu.VMEM((112, LANES), jnp.float32),
            pltpu.SemaphoreType.DMA((len(pieces),)),
            pltpu.SemaphoreType.DMA((bands, OWN)),
        ],
        name="work",
    )(rows, cols, me, sky, halo, *pieces)


def on_device(sky, observed, psf, anchor, offsets):
    bands = sky.shape[0]
    per_device = observed.shape[1]
    n_sky = lax.axis_size("sky")
    n_exp = lax.axis_size("exp")
    slots = n_sky * n_exp
    column = lax.axis_index("sky")
    replica = lax.axis_index("exp")
    parity = column % 2
    both = ("sky", "exp")

    border = lax.dynamic_slice(sky, (0, 0, (1 - parity) * (TILE - LANES)), (bands, sky.shape[1], LANES))
    halo = lax.ppermute(border, "sky", [(s, s ^ 1) for s in range(n_sky)])

    first = (column - parity).astype(jnp.int32)
    anchors = anchor.reshape(bands, slots, per_device)
    row_off = offsets[:, 0].reshape(bands, slots, per_device)
    col_off = offsets[:, 1].reshape(bands, slots, per_device)
    hit = anchors == first
    rows = jnp.sum(jnp.where(hit, row_off, 0), axis=-1)
    cols = jnp.sum(jnp.where(hit, col_off, 0), axis=-1)
    meets = jnp.where(parity == 0, cols < TILE, cols + WIN > TILE)
    present = jnp.any(hit, axis=-1) & meets
    cols = jnp.where(present, cols - parity * (TILE - LANES), -1)
    rows = jnp.where(present, rows, 0)

    blocks = pack(observed, psf)
    if per_device == 1 and n_sky == 4 and n_exp == 2:
        own = blocks.reshape(1, bands, ROWS, LANES)

        def across(x, mask):
            return lax.ppermute(x, both, [(i, i ^ mask) for i in range(slots)])

        far = across(own, 4)
        pieces = [own, far]
        layout = [0, 4]
        for mask in (1, 2, 3):
            pieces += [across(own, mask), across(far, mask)]
            layout += [mask, mask ^ 4]
    else:
        mine = lax.dynamic_index_in_dim(anchors, column * n_exp + replica, 1, keepdims=False)
        pair = 2 * jnp.arange(n_sky // 2, dtype=jnp.int32)[None, :, None]
        chosen = jnp.argmax(mine[:, None, :] == pair, axis=-1)
        picked = jnp.take_along_axis(blocks, chosen[:, :, None, None], axis=1)
        send = jnp.broadcast_to(
            jnp.moveaxis(picked, 1, 0)[:, None], (n_sky // 2, 2 * n_exp, bands, ROWS, LANES)
        ).reshape(slots, bands, ROWS, LANES)
        pieces = [lax.all_to_all(send, both, 0, 0, tiled=True)]
        layout = [None]
    me = jnp.stack([column * n_exp + replica, parity]).astype(jnp.int32)
    return work(rows, cols, me, sky, halo, pieces, layout, slots)


def solution(mesh):
    return jax.shard_map(
        on_device,
        mesh=mesh,
        in_specs=(
            P("band", None, ("group", "sky")),
            P("band", ("group", "sky", "exp"), None, None),
            P("band", ("group", "sky", "exp"), None),
            P("band", "group"),
            P("band", None, "group"),
        ),
        out_specs=P("band", None, ("group", "sky")),
        check_vma=False,
    )
```

```python
import functools

import jax
import jax.numpy as jnp
import numpy as np
from jax import lax
from jax.experimental import pallas as pl
from jax.experimental.pallas import tpu as pltpu
from jax.sharding import PartitionSpec as P

TILE = 256
PSF = 25
STAMP = 64
HALF = STAMP // 2
WIN = 88
LANES = 128
PAIRS = (PSF + 1) // 2
ROWS = 48
WPAD = 96
OWN = TILE // LANES
STRIP = OWN + 1
EDGE = PSF - 1
FOLD = 4
TOGETHER = 2


def lane_of(shape):
    return lax.broadcasted_iota(jnp.int32, shape, 1)


def row_of(shape):
    return lax.broadcasted_iota(jnp.int32, shape, 0)


def spread_table():
    k = np.arange(PSF * PSF) % (2 * PSF)
    place = np.where(k < PSF, -k % LANES, STAMP - (k - PSF))
    return jnp.asarray(place[:, None] == np.arange(LANES)[None, :], jnp.bfloat16)


def prep_kernel(sky_hbm, table_hbm, obs_hbm, psf_hbm, blocks_ref, border_ref, edge, table, obs, psf, sems):
    bands, per_device = obs.shape[:2]
    parity = lax.axis_index("sky") % 2
    side = pl.multiple_of((1 - parity) * (TILE - LANES), LANES)
    copies = [
        pltpu.make_async_copy(src, dst, sems.at[at])
        for at, (src, dst) in enumerate(
            [(psf_hbm, psf), (table_hbm, table), (obs_hbm, obs), (sky_hbm.at[:, :, pl.ds(side, LANES)], edge)]
        )
    ]
    for copy in copies:
        copy.start()
    for copy in copies[:3]:
        copy.wait()
    taps = PSF * PSF
    gap = lane_of((16, taps)) - 2 * PSF * row_of((16, taps))
    inside = (gap >= 0) & (gap < 2 * PSF)
    for b in range(bands):
        for x in range(per_device):
            stamp = obs[b, x].astype(jnp.float32)
            both = jnp.concatenate([stamp[:HALF], stamp[HALF:]], axis=1)
            blocks_ref[x, b, 0:HALF, :] = both.astype(jnp.bfloat16)
            flat = jnp.broadcast_to(psf[b, x : x + 1, :].astype(jnp.float32), (16, taps))
            mine = jnp.where(inside, flat, 0.0).astype(jnp.bfloat16)
            rows = jnp.dot(mine, table[...], preferred_element_type=jnp.float32)
            blocks_ref[x, b, HALF:ROWS, :] = rows.astype(jnp.bfloat16)
    copies[3].wait()
    fold = edge.shape[1] // FOLD
    lane = lane_of((fold, LANES))
    base = (1 - parity) * WIN
    for b in range(bands):
        turned = []
        for g in range(FOLD):
            part = edge[b, g * fold : (g + 1) * fold, :].astype(jnp.float32)
            turned.append(pltpu.roll(part, (base + WIN * g) % LANES, 1))
        for t in range(STRIP):
            limit = WIN * (t + 1) - LANES * t
            tile = jnp.where(lane < limit, turned[t], turned[t + 1])
            border_ref[b, :, t * LANES : (t + 1) * LANES] = tile.astype(jnp.bfloat16)


def prep(sky, observed, psf):
    bands, per_device = observed.shape[:2]
    rows_total = sky.shape[1]
    table = spread_table()
    anywhere = pl.BlockSpec(memory_space=pl.ANY)
    vmem = pl.BlockSpec(memory_space=pltpu.VMEM)
    return pl.pallas_call(
        prep_kernel,
        out_shape=(
            jax.ShapeDtypeStruct((per_device, bands, ROWS, LANES), jnp.bfloat16),
            jax.ShapeDtypeStruct((bands, rows_total // FOLD, STRIP * LANES), jnp.bfloat16),
        ),
        in_specs=[anywhere] * 4,
        out_specs=(vmem, vmem),
        scratch_shapes=[
            pltpu.VMEM((bands, rows_total, LANES), jnp.bfloat16),
            pltpu.VMEM(table.shape, jnp.bfloat16),
            pltpu.VMEM(observed.shape, jnp.bfloat16),
            pltpu.VMEM(psf.shape, jnp.bfloat16),
            pltpu.SemaphoreType.DMA((4,)),
        ],
        name="prep",
    )(sky, table, observed, psf)


def list_jobs(jobs, anchor_ref, offset_ref, column, bands, slots, per_device):
    parity = column % 2
    low = jnp.where(parity == 0, -1, TILE - WIN)
    high = jnp.where(parity == 0, TILE, 2 * TILE)
    count = jnp.int32(0)

    def visit(b, n, count):
        for x in range(per_device):
            i = n * per_device + x
            left = offset_ref[b, 1, i]
            meets = (anchor_ref[b, i] == column - parity) & (left > low) & (left < high)
            jobs[0, count] = jnp.int32(b)
            jobs[1, count] = jnp.int32(n)
            jobs[2, count] = offset_ref[b, 0, i]
            jobs[3, count] = left - parity * (TILE - LANES)
            count = count + meets.astype(jnp.int32)
        return count

    for b in range(bands):
        if slots <= 8:
            for n in range(slots):
                count = visit(b, n, count)
        else:
            count = lax.fori_loop(0, slots, functools.partial(visit, b), count)
    for extra in range(TOGETHER - 1):
        for field in range(4):
            jobs[field, count + extra] = jnp.int32(0)
    return count


def work_kernel(layout, slots, per_device, anchor_ref, offset_ref, sky_hbm, halo_hbm, *rest):
    pieces = rest[: len(layout)]
    rest = rest[len(layout) :]
    out_hbm, jobs, strip, total, halo, blocks, cut, banded, wide, rows_a, rows_r, sems, out_sems = rest
    bands, rows_total = sky_hbm.shape[:2]
    column = lax.axis_index("sky")
    parity = column % 2
    position = column * lax.axis_size("exp") + lax.axis_index("exp")

    copies = [pltpu.make_async_copy(halo_hbm, halo, sems.at[0])]
    for t in range(OWN):
        copies.append(
            pltpu.make_async_copy(
                sky_hbm.at[:, :, pl.ds(t * LANES, LANES)],
                strip.at[:, parity + t, pl.ds(0, rows_total), :],
                sems.at[1 + t],
            )
        )
    at = 1 + OWN
    for masks, piece in zip(layout, pieces):
        if masks is None:
            copies.append(pltpu.make_async_copy(piece, blocks, sems.at[at]))
            at += 1
        else:
            for j, mask in enumerate(masks):
                dst = blocks.at[jnp.bitwise_xor(position, mask)]
                copies.append(pltpu.make_async_copy(piece.at[j], dst, sems.at[at]))
                at += 1
    for copy in copies:
        copy.start()

    count = list_jobs(jobs, anchor_ref, offset_ref, column, bands, slots, per_device)
    rows_r[...] = jnp.zeros(rows_r.shape, jnp.float32)
    for b in range(bands):
        for t in range(OWN):
            total[b, parity + t] = jnp.zeros((rows_total, LANES), jnp.float32)
        for t in range(STRIP):
            strip[b, t, rows_total : rows_total + 16, :] = jnp.zeros((16, LANES), jnp.bfloat16)

    copies[0].wait()
    fold = rows_total // FOLD
    place = parity * (LANES - WIN)
    lane = jnp.bitwise_and(lane_of((fold, LANES)) - place, LANES - 1)
    for b in range(bands):
        tiles = [halo[b, :, t * LANES : (t + 1) * LANES].astype(jnp.float32) for t in range(STRIP)]
        for g in range(FOLD):
            shift = (place + LANES - WIN * g % LANES) % LANES
            first = WIN * g // LANES
            limit = LANES * (first + 1) - WIN * g
            value = pltpu.roll(tiles[first], shift, 1)
            if limit < WIN:
                value = jnp.where(lane < limit, value, pltpu.roll(tiles[first + 1], shift, 1))
            strip[b, OWN * (1 - parity), g * fold : (g + 1) * fold, :] = value.astype(jnp.bfloat16)
    for copy in copies[1:]:
        copy.wait()

    lane_w = lane_of((WPAD, LANES))
    gap = row_of((WPAD, LANES)) - lane_w % STAMP
    inside = (gap >= 0) & (gap < PSF) & (row_of((WPAD, LANES)) < WIN)
    lane_c = lane_of((WPAD + 16, LANES))
    lane_b = lane_of((WIN, LANES))
    low = lane_of((STAMP, LANES)) < STAMP

    def one(job, u):
        b, n, top, start = (jobs[field, job] for field in range(4))
        tile = lax.shift_right_logical(start, 7)
        shift = jnp.bitwise_and(start, LANES - 1)
        after = jnp.minimum(tile + 1, STRIP - 1)
        back_shift = jnp.bitwise_and(LANES - shift, LANES - 1)
        base = pl.multiple_of(jnp.bitwise_and(top, -16), 16)
        left = pltpu.roll(strip[b, tile, pl.ds(base, WPAD + 16), :].astype(jnp.float32), back_shift, 1)
        right = pltpu.roll(strip[b, after, pl.ds(base, WPAD + 16), :].astype(jnp.float32), back_shift, 1)
        cut[u] = jnp.where(lane_c < LANES - shift, left, right)
        window = cut[u, pl.ds(top - base, WPAD), :].astype(jnp.bfloat16)
        taps = blocks[n, b, HALF:ROWS, :].astype(jnp.float32)
        for m in range(PAIRS):
            spread = jnp.broadcast_to(taps[m : m + 1, :], (WPAD, LANES))
            turned = pltpu.roll(spread, 0, 1, stride=1, stride_axis=0)
            banded[u, :, m * LANES : (m + 1) * LANES] = jnp.where(inside, turned, 0.0).astype(jnp.bfloat16)
        product = jnp.dot(window[:, :WPAD], banded[u], preferred_element_type=jnp.float32)
        for m in range(PAIRS):
            wide[u, m] = product[:, m * LANES : (m + 1) * LANES]
        acc = wide[u, 0, 0:72, :]
        for m in range(1, PAIRS):
            acc = acc + wide[u, m, 2 * m : 2 * m + 72, :]
        rows_a[u] = acc
        model = rows_a[u, 0:STAMP, :] + pltpu.roll(rows_a[u, 1 : STAMP + 1, :], STAMP, 1)
        obs = blocks[n, b, 0:HALF, :].astype(jnp.float32)
        obs = jnp.concatenate([obs, pltpu.roll(obs, STAMP, 1)], axis=0)
        residual = (model - obs).astype(jnp.bfloat16).astype(jnp.float32)
        residual = jnp.where(low, residual, 0.0)
        rows_r[u, EDGE : EDGE + STAMP, :] = residual
        rows_r[u, EDGE + STAMP : EDGE + 72, :] = jnp.zeros((8, LANES), jnp.float32)
        upper = pltpu.roll(rows_r[u, EDGE - 1 : EDGE + 71, :], STAMP, 1)
        rows_r[u, EDGE : EDGE + 72, :] = rows_r[u, EDGE : EDGE + 72, :] + upper
        stack = [
            rows_r[u, EDGE - 2 * m : EDGE - 2 * m + WIN, :].astype(jnp.bfloat16) for m in range(PAIRS)
        ]
        back = lax.dot_general(
            jnp.concatenate(stack, axis=1),
            banded[u],
            (((1,), (1,)), ((), ())),
            preferred_element_type=jnp.float32,
        )
        back = back.astype(jnp.bfloat16).astype(jnp.float32)
        back = jnp.concatenate([back, jnp.zeros((WIN, LANES - WPAD), jnp.float32)], axis=1)
        back = pltpu.roll(back, shift, 1)
        live = job < count
        begin = jnp.where(live, shift, LANES)
        end = jnp.where(live, shift, 0)
        total[b, tile, pl.ds(top, WIN), :] += jnp.where(lane_b >= begin, back, 0.0)
        total[b, after, pl.ds(top, WIN), :] += jnp.where(lane_b < end, back, 0.0)

    def step(index, carry):
        for u in range(TOGETHER):
            one(index * TOGETHER + u, u)
        return carry

    lax.fori_loop(0, lax.div(count + TOGETHER - 1, TOGETHER), step, 0)
    outs = [
        pltpu.make_async_copy(
            total.at[b, parity + t], out_hbm.at[b, :, pl.ds(t * LANES, LANES)], out_sems.at[b, t]
        )
        for b in range(bands)
        for t in range(OWN)
    ]
    for copy in outs:
        copy.start()
    for copy in outs:
        copy.wait()


def work(anchor, offsets, sky, halo, pieces, layout, slots, per_device):
    bands, rows_total = sky.shape[:2]
    smem = pl.BlockSpec(memory_space=pltpu.SMEM)
    anywhere = pl.BlockSpec(memory_space=pl.ANY)
    copies = 1 + OWN + sum(1 if masks is None else len(masks) for masks in layout)
    return pl.pallas_call(
        functools.partial(work_kernel, layout, slots, per_device),
        out_shape=jax.ShapeDtypeStruct((bands, rows_total, TILE), jnp.float32),
        in_specs=[smem, smem] + [anywhere] * (2 + len(pieces)),
        out_specs=anywhere,
        scratch_shapes=[
            pltpu.SMEM((4, bands * slots + TOGETHER), jnp.int32),
            pltpu.VMEM((bands, STRIP, rows_total + 16, LANES), jnp.bfloat16),
            pltpu.VMEM((bands, STRIP, rows_total, LANES), jnp.float32),
            pltpu.VMEM(halo.shape, jnp.bfloat16),
            pltpu.VMEM((slots, bands, ROWS, LANES), jnp.bfloat16),
            pltpu.VMEM((TOGETHER, WPAD + 16, LANES), jnp.float32),
            pltpu.VMEM((TOGETHER, WPAD, PAIRS * LANES), jnp.bfloat16),
            pltpu.VMEM((TOGETHER, PAIRS, WPAD, LANES), jnp.float32),
            pltpu.VMEM((TOGETHER, 72, LANES), jnp.float32),
            pltpu.VMEM((TOGETHER, 112, LANES), jnp.float32),
            pltpu.SemaphoreType.DMA((copies,)),
            pltpu.SemaphoreType.DMA((bands, OWN)),
        ],
        name="work",
    )(anchor, offsets, sky, halo, *pieces)


def on_device(sky, observed, psf, anchor, offsets):
    bands = sky.shape[0]
    per_device = observed.shape[1]
    n_sky = lax.axis_size("sky")
    n_exp = lax.axis_size("exp")
    slots = n_sky * n_exp
    both = ("sky", "exp")

    blocks, border = prep(sky, observed, psf)

    def across(x, mask):
        return lax.ppermute(x, both, [(i, i ^ mask) for i in range(slots)])

    if per_device == 1 and n_sky == 4 and n_exp == 2:
        far = across(blocks, 4)
        halo = lax.ppermute(border, "sky", [(s, s ^ 1) for s in range(n_sky)])
        own = jnp.concatenate([blocks, far], axis=0)
        pieces = [own]
        layout = [(0, 4)]
        for mask in (1, 2, 3):
            pieces.append(across(own, mask))
            layout.append((mask, mask ^ 4))
    else:
        halo = lax.ppermute(border, "sky", [(s, s ^ 1) for s in range(n_sky)])
        position = lax.axis_index("sky") * n_exp + lax.axis_index("exp")
        anchors = anchor.reshape(bands, slots, per_device)
        mine = lax.dynamic_index_in_dim(anchors, position, 1, keepdims=False)
        pair = 2 * jnp.arange(n_sky // 2, dtype=jnp.int32)[:, None, None]
        chosen = jnp.argmax(mine[None] == pair, axis=-1)
        picked = jnp.take_along_axis(blocks[None], chosen[:, None, :, None, None], axis=1)
        send = jnp.broadcast_to(picked, (n_sky // 2, 2 * n_exp, bands, ROWS, LANES))
        send = send.reshape(slots, bands, ROWS, LANES)
        pieces = [lax.all_to_all(send, both, 0, 0, tiled=True)]
        layout = [None]
    return work(anchor, offsets, sky, halo, pieces, layout, slots, per_device)


def solution(mesh):
    return jax.shard_map(
        on_device,
        mesh=mesh,
        in_specs=(
            P("band", None, ("group", "sky")),
            P("band", ("group", "sky", "exp"), None, None),
            P("band", ("group", "sky", "exp"), None),
            P("band", "group"),
            P("band", None, "group"),
        ),
        out_specs=P("band", None, ("group", "sky")),
        check_vma=False,
    )
```

```python
import functools

import jax
import jax.numpy as jnp
from jax import lax
from jax.experimental import pallas as pl
from jax.experimental.pallas import tpu as pltpu
from jax.sharding import PartitionSpec as P

TILE = 256
PSF = 25
STAMP = 64
HALF = STAMP // 2
WIN = 88
LANES = 128
PAIRS = (PSF + 1) // 2
ROWS = 40
SHARED = 7
ASIDE = 32
WPAD = 96
OWN = TILE // LANES
STRIP = OWN + 1
EDGE = PSF - 1
FOLD = 4
TOGETHER = 2
FIELD = (9, 9, 7)
AHEAD = 1
PREP_VMEM = 40000 << 10


def lane_of(shape):
    return lax.broadcasted_iota(jnp.int32, shape, 1)


def row_of(shape):
    return lax.broadcasted_iota(jnp.int32, shape, 0)


def pack_into(blocks_ref, at, obs_ref, psf_ref, rows):
    bands, per_device = obs_ref.shape[:2]
    lines = bands * per_device
    taps = PSF * PSF
    lane = lane_of((lines, LANES))
    turn = (lane_of((LANES, LANES)) + row_of((LANES, LANES))) == LANES - 1
    turn = jnp.where(turn, 1.0, 0.0).astype(jnp.bfloat16)
    tiles = []
    for t in range(pl.cdiv(taps, LANES)):
        tile = psf_ref[:, t * LANES : min((t + 1) * LANES, taps)]
        if tile.shape[1] < LANES:
            tile = jnp.concatenate([tile, jnp.zeros((lines, LANES - tile.shape[1]), tile.dtype)], axis=1)
        tiles.append(jnp.dot(tile, turn, preferred_element_type=jnp.float32))

    def run(first, target, count=PSF):
        t, end = first // LANES, (first + count - 1) // LANES
        value = tiles[t] if end == t else jnp.where(lane < LANES // 2, tiles[t], tiles[end])
        value = pltpu.roll(value, (target + first + 1) % LANES, 1)
        return jnp.where(jnp.bitwise_and(target - lane, LANES - 1) < count, value, 0.0)

    for r in range(8):
        row = jnp.zeros((lines, LANES), jnp.float32)
        for m, aside in ((r, 0), (r + SHARED, ASIDE)):
            if r < SHARED and m < PAIRS:
                row = row + run(2 * PSF * m, aside)
                if 2 * m + 1 < PSF:
                    row = row + run(2 * PSF * m + PSF, aside + STAMP)
        rows[r] = row
    for x in range(per_device):
        for b in range(bands):
            stamp = obs_ref[b, x].astype(jnp.float32)
            both = jnp.concatenate([stamp[:HALF], stamp[HALF:]], axis=1)
            blocks_ref[at + x, b, 0:HALF, :] = both.astype(jnp.bfloat16)
            blocks_ref[at + x, b, HALF:ROWS, :] = rows[:, b * per_device + x, :].astype(jnp.bfloat16)


def prep_kernel(sky_hbm, obs_hbm, psf_hbm, first_ref, second_ref, blocks_ref, edge, obs, psf, rows, sems):
    bands, rows_total = sky_hbm.shape[:2]
    parity = lax.axis_index("sky") % 2
    side = pl.multiple_of((1 - parity) * (TILE - LANES), LANES)
    copies = [
        pltpu.make_async_copy(sky_hbm.at[b, :, pl.ds(side, LANES)], edge.at[b], sems.at[b]) for b in range(bands)
    ]
    copies.append(pltpu.make_async_copy(psf_hbm, psf, sems.at[bands]))
    copies.append(pltpu.make_async_copy(obs_hbm, obs, sems.at[bands + 1]))
    for copy in copies:
        copy.start()
    fold = rows_total // FOLD
    lane = lane_of((fold, LANES))
    base = (1 - parity) * WIN
    for b in range(bands):
        copies[b].wait()
        turned = []
        for g in range(FOLD):
            part = edge[b, g * fold : (g + 1) * fold, :].astype(jnp.float32)
            turned.append(pltpu.roll(part, (base + WIN * g) % LANES, 1))
        dst = first_ref.at[b] if b < AHEAD else second_ref.at[b - AHEAD]
        for t in range(STRIP):
            limit = WIN * (t + 1) - LANES * t
            tile = jnp.where(lane < limit, turned[t], turned[t + 1])
            dst[:, t * LANES : (t + 1) * LANES] = tile.astype(jnp.bfloat16)
    for copy in copies[bands:]:
        copy.wait()
    pack_into(blocks_ref, 0, obs, psf, rows)


def prep(sky, observed, psf):
    bands, rows_total = sky.shape[:2]
    per_device = observed.shape[1]
    shape = (rows_total // FOLD, STRIP * LANES)
    hbm = pl.BlockSpec(memory_space=pltpu.HBM)
    vmem = pl.BlockSpec(memory_space=pltpu.VMEM)
    return pl.pallas_call(
        prep_kernel,
        out_shape=(
            jax.ShapeDtypeStruct((AHEAD,) + shape, jnp.bfloat16),
            jax.ShapeDtypeStruct((bands - AHEAD,) + shape, jnp.bfloat16),
            jax.ShapeDtypeStruct((per_device, bands, ROWS, LANES), jnp.bfloat16),
        ),
        in_specs=[hbm] * 3,
        out_specs=(vmem,) * 3,
        scratch_shapes=[
            pltpu.VMEM((bands, rows_total, LANES), jnp.bfloat16),
            pltpu.VMEM(observed.shape, jnp.bfloat16),
            pltpu.VMEM(psf.shape, jnp.bfloat16),
            pltpu.VMEM((8, bands * per_device, LANES), jnp.float32),
            pltpu.SemaphoreType.DMA((bands + 2,)),
        ],
        compiler_params=pltpu.CompilerParams(vmem_limit_bytes=PREP_VMEM),
        cost_estimate=pl.CostEstimate(flops=0, bytes_accessed=1 << 20, transcendentals=0),
        name="prep",
    )(sky, observed, psf)


def merge_kernel(own_ref, obs_ref, psf_ref, both_ref, rows):
    both_ref[0:1] = own_ref[...]
    pack_into(both_ref, 1, obs_ref, psf_ref, rows)


def merge(own, observed, psf):
    vmem = pl.BlockSpec(memory_space=pltpu.VMEM)
    return pl.pallas_call(
        merge_kernel,
        out_shape=jax.ShapeDtypeStruct((2 * own.shape[0],) + own.shape[1:], jnp.bfloat16),
        in_specs=[vmem] * 3,
        out_specs=vmem,
        scratch_shapes=[pltpu.VMEM((8, psf.shape[0], LANES), jnp.float32)],
        compiler_params=pltpu.CompilerParams(vmem_limit_bytes=8 << 20),
        cost_estimate=pl.CostEstimate(flops=0, bytes_accessed=1 << 20, transcendentals=0),
        name="merge",
    )(own, observed, psf)


def plan_kernel(bands, anchor_ref, offset_ref, plan_ref):
    column = lax.axis_index("sky")
    parity = column % 2
    first = column - parity
    crossing = TILE - WIN
    slots = lax.axis_size("sky") * lax.axis_size("exp")
    per_device = anchor_ref.shape[1] // slots
    cap = plan_ref.shape[1]
    low = jnp.where(parity == 0, -1, crossing)
    high = jnp.where(parity == 0, TILE, 2 * TILE)
    aside = parity * (TILE - LANES)

    def code_of(b, n, top, start):
        code = jnp.int32(b << (FIELD[0] + FIELD[1] + FIELD[2]))
        return code + (n << (FIELD[0] + FIELD[1])) + (top << FIELD[1]) + start

    def visit(b, n, counts):
        early, late = counts
        for x in range(per_device):
            i = n * per_device + x
            left = offset_ref[b, 1, i]
            meets = (anchor_ref[b, i] == first) & (left > low) & (left < high)
            code = code_of(b, n, offset_ref[b, 0, i], left - aside)
            if b < AHEAD:
                plan_ref[0, early] = code
                early = early + meets.astype(jnp.int32)
            else:
                later = meets & (left > crossing) & (left < TILE)
                plan_ref[0, early] = code
                plan_ref[1, late] = code
                late = late + later.astype(jnp.int32)
                early = early + (meets.astype(jnp.int32) - later.astype(jnp.int32))
        return early, late

    counts = (jnp.int32(0), jnp.int32(0))
    for b in range(bands):
        if slots <= 8:
            for n in range(slots):
                counts = visit(b, jnp.int32(n), counts)
        else:
            counts = lax.fori_loop(0, slots, functools.partial(visit, b), counts)
    for k in range(2):
        for extra in range(TOGETHER):
            plan_ref[k, counts[k] + extra] = code_of(bands - 1, jnp.int32(0), jnp.int32(0), jnp.int32(LANES))
        plan_ref[k, cap - 1] = counts[k]


def make_plan(anchor, offsets, slots):
    bands = anchor.shape[0]
    smem = pl.BlockSpec(memory_space=pltpu.SMEM)
    return pl.pallas_call(
        functools.partial(plan_kernel, bands),
        out_shape=jax.ShapeDtypeStruct((2, bands * slots + TOGETHER + 2), jnp.int32),
        in_specs=[smem] * 2,
        out_specs=smem,
        compiler_params=pltpu.CompilerParams(vmem_limit_bytes=8 << 20),
        cost_estimate=pl.CostEstimate(flops=0, bytes_accessed=1 << 20, transcendentals=0),
        name="plan",
    )(anchor, offsets)


def unfold(strip, b, tile, halo, place, rows_total):
    fold = rows_total // FOLD
    lane = jnp.bitwise_and(lane_of((fold, LANES)) - place, LANES - 1)
    tiles = [halo[:, t * LANES : (t + 1) * LANES].astype(jnp.float32) for t in range(STRIP)]
    for g in range(FOLD):
        shift = (place + LANES - WIN * g % LANES) % LANES
        first = WIN * g // LANES
        limit = LANES * (first + 1) - WIN * g
        value = pltpu.roll(tiles[first], shift, 1)
        if limit < WIN:
            value = jnp.where(lane < limit, value, pltpu.roll(tiles[first + 1], shift, 1))
        strip[b, tile, g * fold : (g + 1) * fold, :] = value.astype(jnp.bfloat16)


def work_kernel(late, layout, plan_ref, sky_hbm, halo, *rest):
    pieces = rest[: len(layout)]
    rest = rest[len(layout) + late :]
    out_hbm, strip, total, blocks, cut, view, banded, wide, rows_a, rows_r, sems, out_sems = rest
    bands, rows_total = sky_hbm.shape[:2]
    column = lax.axis_index("sky")
    parity = column % 2
    position = column * lax.axis_size("exp") + lax.axis_index("exp")
    border_tile = OWN * (1 - parity)
    mine = list(range(AHEAD if late else 0, bands))
    own = [1 - parity] if late else list(range(OWN))

    def tile_copy(b, t, k):
        side = pl.multiple_of(t * LANES, LANES)
        return pltpu.make_async_copy(
            sky_hbm.at[b, :, pl.ds(side, LANES)], strip.at[b, parity + t, pl.ds(0, rows_total), :], sems.at[b, k]
        )

    def total_copy(b, t, k, inward):
        side = pl.multiple_of(t * LANES, LANES)
        here, there = total.at[b, parity + t], out_hbm.at[b, :, pl.ds(side, LANES)]
        if inward:
            return pltpu.make_async_copy(there, here, out_sems.at[b, k])
        return pltpu.make_async_copy(here, there, out_sems.at[b, k])

    copies = [tile_copy(b, t, k) for b in mine for k, t in enumerate(own)]
    if late:
        copies += [total_copy(b, t, k, True) for b in mine for k, t in enumerate(own)]
    for copy in copies:
        copy.start()
    for masks, piece in zip(layout, pieces):
        if masks is not None:
            for j, mask in enumerate(masks):
                blocks[jnp.bitwise_xor(position, mask)] = piece[j]
        else:
            blocks = piece

    mode = int(late)
    count = plan_ref[mode, plan_ref.shape[1] - 1]
    rows_r[...] = jnp.zeros(rows_r.shape, jnp.float32)
    for b in mine:
        if not late:
            for t in range(OWN):
                total[b, parity + t] = jnp.zeros((rows_total, LANES), jnp.float32)
            if b >= AHEAD:
                strip[b, border_tile, 0:rows_total, :] = jnp.zeros((rows_total, LANES), jnp.bfloat16)
        for t in range(STRIP):
            strip[b, t, rows_total : rows_total + 16, :] = jnp.zeros((16, LANES), jnp.bfloat16)
    for k, b in enumerate(mine if late else range(AHEAD)):
        unfold(strip, b, border_tile, halo[k], parity * (LANES - WIN), rows_total)
    for copy in copies:
        copy.wait()

    lane_w = lane_of((WPAD, LANES))
    gap = row_of((WPAD, LANES)) - lane_w % STAMP
    inside = (gap >= 0) & (gap < PSF) & (row_of((WPAD, LANES)) < WIN)
    lane_c = lane_of((WPAD + 16, LANES))
    lane_b = lane_of((WIN, LANES))
    low = lane_of((STAMP, LANES)) < STAMP

    def where_is(job):
        code = plan_ref[mode, job]
        n = jnp.bitwise_and(lax.shift_right_logical(code, FIELD[0] + FIELD[1]), (1 << FIELD[2]) - 1)
        return lax.shift_right_logical(code, FIELD[0] + FIELD[1] + FIELD[2]), n, code

    def fields(job):
        b, n, code = where_is(job)
        top = jnp.bitwise_and(lax.shift_right_logical(code, FIELD[1]), (1 << FIELD[0]) - 1)
        start = jnp.bitwise_and(code, (1 << FIELD[1]) - 1)
        tile = lax.shift_right_logical(start, 7)
        shift = jnp.bitwise_and(start, LANES - 1)
        after = jnp.minimum(tile + 1, STRIP - 1)
        return b, n, top, tile, after, shift

    def load_window(job, u):
        b, _, top, tile, after, shift = fields(job)
        back_shift = jnp.bitwise_and(LANES - shift, LANES - 1)
        base = pl.multiple_of(jnp.bitwise_and(top, -16), 16)
        left = pltpu.roll(strip[b, tile, pl.ds(base, WPAD + 16), :].astype(jnp.float32), back_shift, 1)
        right = pltpu.roll(strip[b, after, pl.ds(base, WPAD + 16), :].astype(jnp.float32), back_shift, 1)
        cut[u] = jnp.where(lane_c < LANES - shift, left, right)
        view[u] = cut[u, pl.ds(top - base, WPAD), :].astype(jnp.bfloat16)

    def build(job, u, first, last):
        b, n, _ = where_is(job)
        taps = blocks[n, b, HALF:ROWS, :].astype(jnp.float32)
        for m in range(first, min(last, PAIRS)):
            row = m % SHARED
            spread = jnp.broadcast_to(taps[row : row + 1, :], (WPAD, LANES))
            offset = 0 if m < SHARED else LANES - ASIDE
            turned = pltpu.roll(spread, offset, 1, stride=1, stride_axis=0)
            banded[u, :, m * LANES : (m + 1) * LANES] = jnp.where(inside, turned, 0.0).astype(jnp.bfloat16)

    def forward(u, first, last):
        last = min(last, PAIRS)
        product = jnp.dot(
            view[u, :, :WPAD],
            banded[u, :, first * LANES : last * LANES],
            preferred_element_type=jnp.float32,
        )
        for m in range(first, last):
            wide[u, m] = product[:, (m - first) * LANES : (m - first + 1) * LANES]

    def residual(job, u):
        b, n, _ = where_is(job)
        acc = wide[u, 0, 0:72, :]
        for m in range(1, PAIRS):
            acc = acc + wide[u, m, 2 * m : 2 * m + 72, :]
        rows_a[u] = acc
        model = rows_a[u, 0:STAMP, :] + pltpu.roll(rows_a[u, 1 : STAMP + 1, :], STAMP, 1)
        obs = blocks[n, b, 0:HALF, :].astype(jnp.float32)
        obs = jnp.concatenate([obs, pltpu.roll(obs, STAMP, 1)], axis=0)
        rest = (model - obs).astype(jnp.bfloat16).astype(jnp.float32)
        rest = jnp.where(low, rest, 0.0)
        rows_r[u, EDGE : EDGE + STAMP, :] = rest
        rows_r[u, EDGE + STAMP : EDGE + 72, :] = jnp.zeros((8, LANES), jnp.float32)
        upper = pltpu.roll(rows_r[u, EDGE - 1 : EDGE + 71, :], STAMP, 1)
        rows_r[u, EDGE : EDGE + 72, :] = rows_r[u, EDGE : EDGE + 72, :] + upper

    def backward(u):
        stack = [
            rows_r[u, EDGE - 2 * m : EDGE - 2 * m + WIN, :].astype(jnp.bfloat16) for m in range(PAIRS)
        ]
        back = lax.dot_general(
            jnp.concatenate(stack, axis=1),
            banded[u],
            (((1,), (1,)), ((), ())),
            preferred_element_type=jnp.float32,
        )
        back = back.astype(jnp.bfloat16).astype(jnp.float32)
        return jnp.concatenate([back, jnp.zeros((WIN, LANES - WPAD), jnp.float32)], axis=1)

    def add(job, back):
        b, _, top, tile, after, shift = fields(job)
        back = pltpu.roll(back, shift, 1)
        live = job < count
        begin = jnp.where(live, shift, LANES)
        end = jnp.where(live, shift, 0)
        if late:
            from_left = jnp.where(parity == 0, begin, LANES)
            to_right = jnp.where(parity == 0, 0, end)
            part = jnp.where((lane_b >= from_left) | (lane_b < to_right), back, 0.0)
            total[b, 1, pl.ds(top, WIN), :] += part
        else:
            total[b, tile, pl.ds(top, WIN), :] += jnp.where(lane_b >= begin, back, 0.0)
            total[b, after, pl.ds(top, WIN), :] += jnp.where(lane_b < end, back, 0.0)

    outs = {b: [total_copy(b, t, k, False) for k, t in enumerate(own)] for b in mine}

    def flush(b, ready):
        @pl.when(ready)
        def _():
            for copy in outs[b]:
                copy.start()

    def step(index, before):
        one = index * 2
        two = one + 1
        now = where_is(one)[0]
        for b in mine[:-1]:
            flush(b, (before <= b) & (now > b))
        load_window(two, 1)
        for c in range(0, PAIRS, 2):
            forward(0, c, c + 2)
            build(two, 1, c, c + 2)
        residual(one, 0)
        for c in range(0, PAIRS, 2):
            forward(1, c, c + 2)
        back_one = backward(0)
        residual(two, 1)
        back_two = backward(1)
        add(one, back_one)
        load_window(one + 2, 0)
        build(one + 2, 0, 0, PAIRS)
        add(two, back_two)
        return now

    load_window(0, 0)
    build(0, 0, 0, PAIRS)
    before = lax.fori_loop(0, lax.div(count + 1, 2), step, jnp.int32(0))
    for b in mine:
        flush(b, before <= b)
    for b in mine:
        for copy in outs[b]:
            copy.wait()


def work(late, plan, sky, halo, pieces, layout, slots, so_far=None):
    bands, rows_total = sky.shape[:2]
    smem = pl.BlockSpec(memory_space=pltpu.SMEM)
    hbm = pl.BlockSpec(memory_space=pltpu.HBM)
    vmem = pl.BlockSpec(memory_space=pltpu.VMEM)
    gathered = (slots, bands, ROWS, LANES) if layout[0] is not None else (1, 1, 8, LANES)
    extra = [so_far] if late else []
    return pl.pallas_call(
        functools.partial(work_kernel, late, layout),
        out_shape=jax.ShapeDtypeStruct((bands, rows_total, TILE), jnp.float32),
        in_specs=[smem, hbm] + [vmem] * (1 + len(pieces)) + [hbm] * len(extra),
        out_specs=hbm,
        scratch_shapes=[
            pltpu.VMEM((bands, STRIP, rows_total + 16, LANES), jnp.bfloat16),
            pltpu.VMEM((bands, STRIP, rows_total, LANES), jnp.float32),
            pltpu.VMEM(gathered, jnp.bfloat16),
            pltpu.VMEM((TOGETHER, WPAD + 16, LANES), jnp.float32),
            pltpu.VMEM((TOGETHER, WPAD, LANES), jnp.bfloat16),
            pltpu.VMEM((TOGETHER, WPAD, PAIRS * LANES), jnp.bfloat16),
            pltpu.VMEM((TOGETHER, PAIRS, WPAD, LANES), jnp.float32),
            pltpu.VMEM((TOGETHER, 72, LANES), jnp.float32),
            pltpu.VMEM((TOGETHER, 112, LANES), jnp.float32),
            pltpu.SemaphoreType.DMA((bands, OWN)),
            pltpu.SemaphoreType.DMA((bands, OWN)),
        ],
        compiler_params=pltpu.CompilerParams(vmem_limit_bytes=24 << 20),
        cost_estimate=pl.CostEstimate(flops=0, bytes_accessed=8 << 20, transcendentals=0),
        input_output_aliases={3 + len(pieces): 0} if late else {},
        name="late" if late else "early",
    )(plan, sky, halo, *pieces, *extra)


def on_device(sky, observed, psf, anchor, offsets):
    bands = sky.shape[0]
    per_device = observed.shape[1]
    n_sky = lax.axis_size("sky")
    n_exp = lax.axis_size("exp")
    slots = n_sky * n_exp
    both = ("sky", "exp")
    taps = psf.reshape(bands * per_device, psf.shape[-1])
    direct = per_device == 1 and n_sky == 4 and n_exp == 2

    def across(x, mask):
        return lax.ppermute(x, both, [(i, i ^ mask) for i in range(slots)])

    def neighbour(x):
        return lax.ppermute(x, "sky", [(s, s ^ 1) for s in range(n_sky)])

    if direct:
        far_observed = across(observed, 4)
        far_taps = across(taps, 4)
    first, second, blocks = prep(sky, observed, taps)
    halo_first = neighbour(first)
    if direct:
        own = merge(blocks, far_observed, far_taps)
        pieces = [own]
        layout = [(0, 4)]
        for mask in (2, 3, 1):
            pieces.append(across(own, mask))
            layout.append((mask, mask ^ 4))
    else:
        position = lax.axis_index("sky") * n_exp + lax.axis_index("exp")
        anchors = anchor.reshape(bands, slots, per_device)
        mine = lax.dynamic_index_in_dim(anchors, position, 1, keepdims=False)
        pair = 2 * jnp.arange(n_sky // 2, dtype=jnp.int32)[:, None, None]
        chosen = jnp.argmax(mine[None] == pair, axis=-1)
        picked = jnp.take_along_axis(blocks[None], chosen[:, None, :, None, None], axis=1)
        send = jnp.broadcast_to(picked, (n_sky // 2, 2 * n_exp, bands, ROWS, LANES))
        send = send.reshape(slots, bands, ROWS, LANES)
        pieces = [lax.all_to_all(send, both, 0, 0, tiled=True)]
        layout = [None]
    halo_second = neighbour(second)
    plan = make_plan(anchor, offsets, slots)
    so_far = work(False, plan, sky, halo_first, pieces, layout, slots)
    return work(True, plan, sky, halo_second, pieces, layout, slots, so_far)


def solution(mesh):
    return jax.shard_map(
        on_device,
        mesh=mesh,
        in_specs=(
            P("band", None, ("group", "sky")),
            P("band", ("group", "sky", "exp"), None, None),
            P("band", ("group", "sky", "exp"), None),
            P("band", "group"),
            P("band", None, "group"),
        ),
        out_specs=P("band", None, ("group", "sky")),
        check_vma=False,
    )
```

```python
import functools

import jax
import jax.numpy as jnp
from jax import lax
from jax.experimental import pallas as pl
from jax.experimental.pallas import tpu as pltpu
from jax.sharding import PartitionSpec as P

TILE = 256
PSF = 25
STAMP = 64
HALF = STAMP // 2
WIN = 88
LANES = 128
PAIRS = (PSF + 1) // 2
ROWS = 40
SHARED = 7
ASIDE = 32
WPAD = 96
OWN = TILE // LANES
FOLDED = 3
EDGE = PSF - 1
FOLD = 4
TOGETHER = 2
FIELD = (9, 9, 7)
SMALL_VMEM = 8 << 20
WORK_VMEM = 24 << 20
CUT = 120


def lane_of(shape):
    return lax.broadcasted_iota(jnp.int32, shape, 1)


def row_of(shape):
    return lax.broadcasted_iota(jnp.int32, shape, 0)


def pack_into(blocks_ref, at, obs_ref, psf_ref, rows):
    bands, per_device = obs_ref.shape[:2]
    lines = bands * per_device
    taps = PSF * PSF
    lane = lane_of((lines, LANES))
    turn = (lane_of((LANES, LANES)) + row_of((LANES, LANES))) == LANES - 1
    turn = jnp.where(turn, 1.0, 0.0).astype(jnp.bfloat16)
    tiles = []
    for t in range(pl.cdiv(taps, LANES)):
        tile = psf_ref[:, t * LANES : min((t + 1) * LANES, taps)]
        if tile.shape[1] < LANES:
            tile = jnp.concatenate([tile, jnp.zeros((lines, LANES - tile.shape[1]), tile.dtype)], axis=1)
        tiles.append(jnp.dot(tile, turn, preferred_element_type=jnp.float32))

    def run(first, target, count=PSF):
        t, end = first // LANES, (first + count - 1) // LANES
        value = tiles[t] if end == t else jnp.where(lane < LANES // 2, tiles[t], tiles[end])
        value = pltpu.roll(value, (target + first + 1) % LANES, 1)
        return jnp.where(jnp.bitwise_and(target - lane, LANES - 1) < count, value, 0.0)

    for r in range(8):
        row = jnp.zeros((lines, LANES), jnp.float32)
        for m, aside in ((r, 0), (r + SHARED, ASIDE)):
            if r < SHARED and m < PAIRS:
                row = row + run(2 * PSF * m, aside)
                if 2 * m + 1 < PSF:
                    row = row + run(2 * PSF * m + PSF, aside + STAMP)
        rows[r] = row
    for x in range(per_device):
        for b in range(bands):
            stamp = obs_ref[b, x].astype(jnp.float32)
            both = jnp.concatenate([stamp[:HALF], stamp[HALF:]], axis=1)
            blocks_ref[at + x, b, 0:HALF, :] = both.astype(jnp.bfloat16)
            blocks_ref[at + x, b, HALF:ROWS, :] = rows[:, b * per_device + x, :].astype(jnp.bfloat16)


def prep_kernel(
    sky_hbm, obs_hbm, psf_hbm, anchor_hbm, offset_hbm,
    sky_ref, border_ref, blocks_ref, plan_ref,
    obs, psf, anchor, offset, rows, sems,
):
    bands, rows_total = sky_hbm.shape[:2]
    parity = lax.axis_index("sky") % 2
    copies = []

    def bring(src, dst):
        copies.append(pltpu.make_async_copy(src, dst, sems.at[len(copies)]))

    bring(anchor_hbm, anchor)
    bring(offset_hbm, offset)
    for b in range(bands):
        for t in range(OWN):
            bring(sky_hbm.at[b, :, pl.ds(t * LANES, LANES)], sky_ref.at[b, t])
    bring(psf_hbm, psf)
    bring(obs_hbm, obs)
    for copy in copies:
        copy.start()
    copies[0].wait()
    copies[1].wait()
    list_windows(anchor, offset, plan_ref, bands)
    fold = rows_total // FOLD
    lane = lane_of((fold, LANES))
    base = (1 - parity) * WIN
    for b in range(bands):
        for t in range(OWN):
            copies[2 + b * OWN + t].wait()
        turned = []
        for g in range(FOLD):
            part = sky_ref[b, 1 - parity, g * fold : (g + 1) * fold, :].astype(jnp.float32)
            turned.append(pltpu.roll(part, (base + WIN * g) % LANES, 1))
        for t in range(FOLDED):
            limit = WIN * (t + 1) - LANES * t
            tile = jnp.where(lane < limit, turned[t], turned[t + 1])
            border_ref[b, :, t * LANES : (t + 1) * LANES] = tile.astype(jnp.bfloat16)
    for copy in copies[2 + bands * OWN :]:
        copy.wait()
    pack_into(blocks_ref, 0, obs, psf, rows)


def prep(sky, observed, psf, anchor, offsets, slots):
    bands, rows_total = sky.shape[:2]
    per_device = observed.shape[1]
    hbm = pl.BlockSpec(memory_space=pltpu.HBM)
    vmem = pl.BlockSpec(memory_space=pltpu.VMEM)
    smem = pl.BlockSpec(memory_space=pltpu.SMEM)
    arrays = [pltpu.with_memory_space_constraint(x, pltpu.HBM) for x in (sky, observed, psf, anchor, offsets)]
    return pl.pallas_call(
        prep_kernel,
        out_shape=(
            jax.ShapeDtypeStruct((bands, OWN, rows_total, LANES), jnp.bfloat16),
            jax.ShapeDtypeStruct((bands, rows_total // FOLD, FOLDED * LANES), jnp.bfloat16),
            jax.ShapeDtypeStruct((per_device, bands, ROWS, LANES), jnp.bfloat16),
            jax.ShapeDtypeStruct((2, bands * slots + TOGETHER + 2), jnp.int32),
        ),
        in_specs=[hbm] * 5,
        out_specs=(vmem, vmem, vmem, smem),
        scratch_shapes=[
            pltpu.VMEM(observed.shape, jnp.bfloat16),
            pltpu.VMEM(psf.shape, jnp.bfloat16),
            pltpu.SMEM(anchor.shape, jnp.int32),
            pltpu.SMEM(offsets.shape, jnp.int32),
            pltpu.VMEM((8, bands * per_device, LANES), jnp.float32),
            pltpu.SemaphoreType.DMA((bands * OWN + 4,)),
        ],
        compiler_params=pltpu.CompilerParams(vmem_limit_bytes=SMALL_VMEM),
        cost_estimate=pl.CostEstimate(flops=0, bytes_accessed=1 << 20, transcendentals=0),
        name="prep",
    )(*arrays)


def merge_kernel(own_ref, obs_ref, psf_ref, both_ref, rows):
    both_ref[0:1] = own_ref[...]
    pack_into(both_ref, 1, obs_ref, psf_ref, rows)


def merge(own, observed, psf):
    vmem = pl.BlockSpec(memory_space=pltpu.VMEM)
    return pl.pallas_call(
        merge_kernel,
        out_shape=jax.ShapeDtypeStruct((2 * own.shape[0],) + own.shape[1:], jnp.bfloat16),
        in_specs=[vmem] * 3,
        out_specs=vmem,
        scratch_shapes=[pltpu.VMEM((8, psf.shape[0], LANES), jnp.float32)],
        compiler_params=pltpu.CompilerParams(vmem_limit_bytes=SMALL_VMEM),
        cost_estimate=pl.CostEstimate(flops=0, bytes_accessed=1 << 20, transcendentals=0),
        name="merge",
    )(own, observed, psf)


def list_windows(anchor_ref, offset_ref, plan_ref, bands):
    column = lax.axis_index("sky")
    parity = column % 2
    first = column - parity
    slots = lax.axis_size("sky") * lax.axis_size("exp")
    per_device = anchor_ref.shape[1] // slots
    cap = plan_ref.shape[1]
    begin = parity * TILE

    def code_of(b, n, top, start):
        code = jnp.int32(b << (FIELD[0] + FIELD[1] + FIELD[2]))
        return code + (n << (FIELD[0] + FIELD[1])) + (top << FIELD[1]) + start

    def visit(b, n, counts):
        inner, cross = counts
        for x in range(per_device):
            i = n * per_device + x
            left = offset_ref[b, 1, i]
            here = anchor_ref[b, i] == first
            code = code_of(b, n, offset_ref[b, 0, i], left)
            plan_ref[0, inner] = code - begin
            plan_ref[1, cross] = code - (TILE - LANES)
            start = left - begin
            inner = inner + (here & (start >= 0) & (start <= TILE - WIN)).astype(jnp.int32)
            cross = cross + (here & (left > TILE - WIN) & (left < TILE)).astype(jnp.int32)
        return inner, cross

    counts = (jnp.int32(0), jnp.int32(0))
    for b in range(bands):
        if slots <= 8:
            for n in range(slots):
                counts = visit(b, jnp.int32(n), counts)
        else:
            counts = lax.fori_loop(0, slots, functools.partial(visit, b), counts)
    for k in range(2):
        for extra in range(TOGETHER):
            plan_ref[k, counts[k] + extra] = code_of(bands - 1, jnp.int32(0), jnp.int32(0), jnp.int32(0))
        plan_ref[k, cap - 1] = counts[k]


def unfold(halo, border_ref, b, place, rows_total):
    fold = rows_total // FOLD
    lane = jnp.bitwise_and(lane_of((fold, LANES)) - place, LANES - 1)
    tiles = [border_ref[b, :, t * LANES : (t + 1) * LANES].astype(jnp.float32) for t in range(FOLDED)]
    for g in range(FOLD):
        shift = (place + LANES - WIN * g % LANES) % LANES
        first = WIN * g // LANES
        limit = LANES * (first + 1) - WIN * g
        value = pltpu.roll(tiles[first], shift, 1)
        if limit < WIN:
            value = jnp.where(lane < limit, value, pltpu.roll(tiles[first + 1], shift, 1))
        halo[b, g * fold : (g + 1) * fold, :] = value.astype(jnp.bfloat16)


def work_kernel(late, layout, plan_ref, sky_ref, *rest):
    if late:
        border_ref, near_ref, *rest = rest
    pieces = rest[: len(layout)]
    rest = rest[len(layout) + late :]
    if late:
        out_hbm, halo, *rest = rest
    else:
        out_hbm, near_ref, *rest = rest
    total, blocks, cut, view, banded, wide, rows_a, rows_r, out_sems = rest
    bands, _, rows_total = sky_ref.shape[:3]
    column = lax.axis_index("sky")
    parity = column % 2
    position = column * lax.axis_size("exp") + lax.axis_index("exp")
    mode = int(late)
    mine = list(range(bands))
    for masks, piece in zip(layout, pieces):
        if masks is not None:
            for j, mask in enumerate(masks):
                blocks[jnp.bitwise_xor(position, mask)] = piece[j]
        else:
            blocks = piece
    count = plan_ref[mode, plan_ref.shape[1] - 1]
    rows_r[...] = jnp.zeros(rows_r.shape, jnp.float32)
    for u in range(TOGETHER):
        cut[u, CUT - 8 : CUT, :] = jnp.zeros((8, LANES), jnp.float32)
    for b in mine:
        if late:
            total[b, 0] = near_ref[b]
            unfold(halo, border_ref, b, parity * (LANES - WIN), rows_total)
        else:
            for t in range(OWN):
                total[b, t] = jnp.zeros((rows_total, LANES), jnp.float32)

    lane_w = lane_of((WPAD, LANES))
    gap = row_of((WPAD, LANES)) - lane_w % STAMP
    inside = (gap >= 0) & (gap < PSF) & (row_of((WPAD, LANES)) < WIN)
    lane_c = lane_of((CUT - 8, LANES))
    lane_b = lane_of((WIN, LANES))
    low = lane_of((STAMP, LANES)) < STAMP

    def where_is(job):
        code = plan_ref[mode, job]
        n = jnp.bitwise_and(lax.shift_right_logical(code, FIELD[0] + FIELD[1]), (1 << FIELD[2]) - 1)
        return lax.shift_right_logical(code, FIELD[0] + FIELD[1] + FIELD[2]), n, code

    def fields(job):
        b, n, code = where_is(job)
        top = jnp.bitwise_and(lax.shift_right_logical(code, FIELD[1]), (1 << FIELD[0]) - 1)
        start = jnp.bitwise_and(code, (1 << FIELD[1]) - 1)
        tile = lax.shift_right_logical(start, 7)
        shift = jnp.bitwise_and(start, LANES - 1)
        return b, n, top, tile, shift

    def load_window(job, u):
        b, _, top, tile, shift = fields(job)
        back_shift = jnp.bitwise_and(LANES - shift, LANES - 1)
        base = pl.multiple_of(jnp.minimum(jnp.bitwise_and(top, -16), rows_total - (CUT - 8)), 16)
        span = pl.ds(base, CUT - 8)
        if late:
            own = pltpu.roll(sky_ref[b, 1 - parity, span, :].astype(jnp.float32), back_shift, 1)
            other = pltpu.roll(halo[b, span, :].astype(jnp.float32), back_shift, 1)
            own_from = jnp.where(parity == 0, 0, LANES - shift)
            own_to = jnp.where(parity == 0, LANES - shift, LANES)
            window = jnp.where((lane_c >= own_from) & (lane_c < own_to), own, other)
        else:
            after = jnp.minimum(tile + 1, OWN - 1)
            left = pltpu.roll(sky_ref[b, tile, span, :].astype(jnp.float32), back_shift, 1)
            right = pltpu.roll(sky_ref[b, after, span, :].astype(jnp.float32), back_shift, 1)
            window = jnp.where(lane_c < LANES - shift, left, right)
        cut[u, 0 : CUT - 8, :] = window
        view[u] = cut[u, pl.ds(top - base, WPAD), :].astype(jnp.bfloat16)

    def build(job, u, first, last):
        b, n, _ = where_is(job)
        taps = blocks[n, b, HALF:ROWS, :].astype(jnp.float32)
        for m in range(first, min(last, PAIRS)):
            row = m % SHARED
            spread = jnp.broadcast_to(taps[row : row + 1, :], (WPAD, LANES))
            offset = 0 if m < SHARED else LANES - ASIDE
            turned = pltpu.roll(spread, offset, 1, stride=1, stride_axis=0)
            banded[u, :, m * LANES : (m + 1) * LANES] = jnp.where(inside, turned, 0.0).astype(jnp.bfloat16)

    def forward(u, first, last):
        last = min(last, PAIRS)
        product = jnp.dot(
            view[u, :, :WPAD],
            banded[u, :, first * LANES : last * LANES],
            preferred_element_type=jnp.float32,
        )
        for m in range(first, last):
            wide[u, m] = product[:, (m - first) * LANES : (m - first + 1) * LANES]

    def residual(job, u):
        b, n, _ = where_is(job)
        acc = wide[u, 0, 0:72, :]
        for m in range(1, PAIRS):
            acc = acc + wide[u, m, 2 * m : 2 * m + 72, :]
        rows_a[u] = acc
        model = rows_a[u, 0:STAMP, :] + pltpu.roll(rows_a[u, 1 : STAMP + 1, :], STAMP, 1)
        obs = blocks[n, b, 0:HALF, :].astype(jnp.float32)
        obs = jnp.concatenate([obs, pltpu.roll(obs, STAMP, 1)], axis=0)
        rest = (model - obs).astype(jnp.bfloat16).astype(jnp.float32)
        rest = jnp.where(low, rest, 0.0)
        rows_r[u, EDGE : EDGE + STAMP, :] = rest
        rows_r[u, EDGE + STAMP : EDGE + 72, :] = jnp.zeros((8, LANES), jnp.float32)
        upper = pltpu.roll(rows_r[u, EDGE - 1 : EDGE + 71, :], STAMP, 1)
        rows_r[u, EDGE : EDGE + 72, :] = rows_r[u, EDGE : EDGE + 72, :] + upper

    def backward(u):
        stack = [
            rows_r[u, EDGE - 2 * m : EDGE - 2 * m + WIN, :].astype(jnp.bfloat16) for m in range(PAIRS)
        ]
        back = lax.dot_general(
            jnp.concatenate(stack, axis=1),
            banded[u],
            (((1,), (1,)), ((), ())),
            preferred_element_type=jnp.float32,
        )
        back = back.astype(jnp.bfloat16).astype(jnp.float32)
        return jnp.concatenate([back, jnp.zeros((WIN, LANES - WPAD), jnp.float32)], axis=1)

    def add(job, back):
        b, _, top, tile, shift = fields(job)
        back = pltpu.roll(back, shift, 1)
        live = job < count
        begin = jnp.where(live, shift, LANES)
        end = jnp.where(live, shift, 0)
        here = pl.ds(top, WIN)
        if late:
            own_from = jnp.where(parity == 0, begin, 0)
            own_to = jnp.where(parity == 0, LANES, end)
            total[b, 0, here, :] += jnp.where((lane_b >= own_from) & (lane_b < own_to), back, 0.0)
        else:
            after = jnp.minimum(tile + 1, OWN - 1)
            total[b, tile, here, :] += jnp.where(lane_b >= begin, back, 0.0)
            total[b, after, here, :] += jnp.where(lane_b < end, back, 0.0)

    def out_copy(b):
        side = pl.multiple_of(jnp.where(late, 1 - parity, parity) * LANES, LANES)
        src = total.at[b, 0] if late else total.at[b, parity]
        return pltpu.make_async_copy(src, out_hbm.at[b, :, pl.ds(side, LANES)], out_sems.at[b])

    outs = {b: [out_copy(b)] for b in mine}

    def flush(b, ready):
        @pl.when(ready)
        def _():
            for copy in outs[b]:
                copy.start()

    def step(index, before):
        one = index * 2
        two = one + 1
        now = where_is(one)[0]
        for b in mine[:-1]:
            flush(b, (before <= b) & (now > b))
        load_window(two, 1)
        for c in range(0, PAIRS, 2):
            forward(0, c, c + 2)
            build(two, 1, c, c + 2)
        residual(one, 0)
        for c in range(0, PAIRS, 2):
            forward(1, c, c + 2)
        back_one = backward(0)
        residual(two, 1)
        back_two = backward(1)
        add(one, back_one)
        load_window(one + 2, 0)
        build(one + 2, 0, 0, PAIRS)
        add(two, back_two)
        return now

    load_window(0, 0)
    build(0, 0, 0, PAIRS)
    before = lax.fori_loop(0, lax.div(count + 1, 2), step, jnp.int32(0))
    for b in mine:
        flush(b, before <= b)
    if not late:
        for b in mine:
            near_ref[b] = total[b, 1 - parity]
    for b in mine:
        for copy in outs[b]:
            copy.wait()


def work(late, plan, sky, pieces, layout, slots, border=None, near=None, so_far=None):
    bands, _, rows_total = sky.shape[:3]
    smem = pl.BlockSpec(memory_space=pltpu.SMEM)
    hbm = pl.BlockSpec(memory_space=pltpu.HBM)
    vmem = pl.BlockSpec(memory_space=pltpu.VMEM)
    gathered = (slots, bands, ROWS, LANES) if layout[0] is not None else (1, 1, 8, LANES)
    gradient = jax.ShapeDtypeStruct((bands, rows_total, TILE), jnp.float32)
    first = [border, near] if late else []
    last = [so_far] if late else []
    return pl.pallas_call(
        functools.partial(work_kernel, late, layout),
        out_shape=gradient if late else (gradient, jax.ShapeDtypeStruct((bands, rows_total, LANES), jnp.float32)),
        in_specs=[smem, vmem] + [vmem] * (len(first) + len(pieces)) + [hbm] * len(last),
        out_specs=hbm if late else (hbm, vmem),
        scratch_shapes=([pltpu.VMEM((bands, rows_total, LANES), jnp.bfloat16)] if late else [])
        + [
            pltpu.VMEM((bands, 1 if late else OWN, rows_total, LANES), jnp.float32),
            pltpu.VMEM(gathered, jnp.bfloat16),
            pltpu.VMEM((TOGETHER, CUT, LANES), jnp.float32),
            pltpu.VMEM((TOGETHER, WPAD, LANES), jnp.bfloat16),
            pltpu.VMEM((TOGETHER, WPAD, PAIRS * LANES), jnp.bfloat16),
            pltpu.VMEM((TOGETHER, PAIRS, WPAD, LANES), jnp.float32),
            pltpu.VMEM((TOGETHER, 72, LANES), jnp.float32),
            pltpu.VMEM((TOGETHER, 112, LANES), jnp.float32),
            pltpu.SemaphoreType.DMA((bands,)),
        ],
        compiler_params=pltpu.CompilerParams(vmem_limit_bytes=WORK_VMEM),
        cost_estimate=pl.CostEstimate(flops=0, bytes_accessed=8 << 20, transcendentals=0),
        input_output_aliases={4 + len(pieces): 0} if late else {},
        name="late" if late else "early",
    )(plan, sky, *first, *pieces, *last)


def on_device(sky, observed, psf, anchor, offsets):
    bands = sky.shape[0]
    per_device = observed.shape[1]
    n_sky = lax.axis_size("sky")
    n_exp = lax.axis_size("exp")
    slots = n_sky * n_exp
    both = ("sky", "exp")
    taps = psf.reshape(bands * per_device, psf.shape[-1])
    direct = per_device == 1 and n_sky == 4 and n_exp == 2

    def across(x, mask):
        return lax.ppermute(x, both, [(i, i ^ mask) for i in range(slots)])

    def neighbour(x):
        return lax.ppermute(x, "sky", [(s, s ^ 1) for s in range(n_sky)])

    if direct:
        far_observed = across(observed, 4)
        far_taps = across(taps, 4)
    tiles, border, blocks, plan = prep(sky, observed, taps, anchor, offsets, slots)
    if direct:
        own = merge(blocks, far_observed, far_taps)
        pieces = [own]
        layout = [(0, 4)]
        for mask in (2, 3, 1):
            pieces.append(across(own, mask))
            layout.append((mask, mask ^ 4))
    else:
        position = lax.axis_index("sky") * n_exp + lax.axis_index("exp")
        anchors = anchor.reshape(bands, slots, per_device)
        mine = lax.dynamic_index_in_dim(anchors, position, 1, keepdims=False)
        pair = 2 * jnp.arange(n_sky // 2, dtype=jnp.int32)[:, None, None]
        chosen = jnp.argmax(mine[None] == pair, axis=-1)
        picked = jnp.take_along_axis(blocks[None], chosen[:, None, :, None, None], axis=1)
        send = jnp.broadcast_to(picked, (n_sky // 2, 2 * n_exp, bands, ROWS, LANES))
        send = send.reshape(slots, bands, ROWS, LANES)
        pieces = [lax.all_to_all(send, both, 0, 0, tiled=True)]
        layout = [None]
    halo = neighbour(border)
    so_far, near = work(False, plan, tiles, pieces, layout, slots)
    return work(True, plan, tiles, pieces, layout, slots, halo, near, so_far)


def solution(mesh):
    return jax.shard_map(
        on_device,
        mesh=mesh,
        in_specs=(
            P("band", None, ("group", "sky")),
            P("band", ("group", "sky", "exp"), None, None),
            P("band", ("group", "sky", "exp"), None),
            P("band", "group"),
            P("band", None, "group"),
        ),
        out_specs=P("band", None, ("group", "sky")),
        check_vma=False,
    )
```

```python
import functools

import jax
import jax.numpy as jnp
from jax import lax
from jax.experimental import pallas as pl
from jax.experimental.pallas import tpu as pltpu
from jax.sharding import PartitionSpec as P

TILE = 256
PSF = 25
STAMP = 64
HALF = STAMP // 2
WIN = 88
LANES = 128
PAIRS = (PSF + 1) // 2
ROWS = 40
SHARED = 7
ASIDE = 32
WPAD = 96
OWN = TILE // LANES
FOLDED = 3
EDGE = PSF - 1
FOLD = 4
TOGETHER = 2
MODES = 3
AHEAD = 1
FIELD = (9, 9, 7)
SMALL_VMEM = 8 << 20
WORK_VMEM = 24 << 20
CUT = 120


def lane_of(shape):
    return lax.broadcasted_iota(jnp.int32, shape, 1)


def row_of(shape):
    return lax.broadcasted_iota(jnp.int32, shape, 0)


def pack_into(blocks_ref, at, obs_ref, psf_ref, rows):
    bands, per_device = obs_ref.shape[:2]
    lines = bands * per_device
    taps = PSF * PSF
    lane = lane_of((lines, LANES))
    turn = (lane_of((LANES, LANES)) + row_of((LANES, LANES))) == LANES - 1
    turn = jnp.where(turn, 1.0, 0.0).astype(jnp.bfloat16)
    tiles = []
    for t in range(pl.cdiv(taps, LANES)):
        tile = psf_ref[:, t * LANES : min((t + 1) * LANES, taps)]
        if tile.shape[1] < LANES:
            tile = jnp.concatenate([tile, jnp.zeros((lines, LANES - tile.shape[1]), tile.dtype)], axis=1)
        tiles.append(jnp.dot(tile, turn, preferred_element_type=jnp.float32))

    def run(first, target, count=PSF):
        t, end = first // LANES, (first + count - 1) // LANES
        value = tiles[t] if end == t else jnp.where(lane < LANES // 2, tiles[t], tiles[end])
        value = pltpu.roll(value, (target + first + 1) % LANES, 1)
        return jnp.where(jnp.bitwise_and(target - lane, LANES - 1) < count, value, 0.0)

    for r in range(8):
        row = jnp.zeros((lines, LANES), jnp.float32)
        for m, aside in ((r, 0), (r + SHARED, ASIDE)):
            if r < SHARED and m < PAIRS:
                row = row + run(2 * PSF * m, aside)
                if 2 * m + 1 < PSF:
                    row = row + run(2 * PSF * m + PSF, aside + STAMP)
        rows[r] = row
    for x in range(per_device):
        for b in range(bands):
            stamp = obs_ref[b, x].astype(jnp.float32)
            both = jnp.concatenate([stamp[:HALF], stamp[HALF:]], axis=1)
            blocks_ref[at + x, b, 0:HALF, :] = both.astype(jnp.bfloat16)
            blocks_ref[at + x, b, HALF:ROWS, :] = rows[:, b * per_device + x, :].astype(jnp.bfloat16)


def prep_kernel(
    distant, sky_hbm, obs_hbm, psf_hbm, anchor_hbm, offset_hbm,
    sky_ref, first_ref, second_ref, blocks_ref, plan_ref,
    obs, psf, anchor, offset, rows, sems,
):
    bands, rows_total = sky_hbm.shape[:2]
    parity = lax.axis_index("sky") % 2
    copies = []

    def bring(src, dst):
        copies.append(pltpu.make_async_copy(src, dst, sems.at[len(copies)]))

    bring(anchor_hbm, anchor)
    bring(offset_hbm, offset)
    for b in range(bands):
        for t in range(OWN):
            bring(sky_hbm.at[b, :, pl.ds(t * LANES, LANES)], sky_ref.at[b, t])
    bring(psf_hbm, psf)
    bring(obs_hbm, obs)
    for copy in copies:
        copy.start()
    copies[0].wait()
    copies[1].wait()
    list_windows(anchor, offset, plan_ref, bands, distant)
    fold = rows_total // FOLD
    lane = lane_of((fold, LANES))
    base = (1 - parity) * WIN
    for b in range(bands):
        for t in range(OWN):
            copies[2 + b * OWN + t].wait()
        turned = []
        for g in range(FOLD):
            part = sky_ref[b, 1 - parity, g * fold : (g + 1) * fold, :].astype(jnp.float32)
            turned.append(pltpu.roll(part, (base + WIN * g) % LANES, 1))
        for t in range(FOLDED):
            limit = WIN * (t + 1) - LANES * t
            tile = jnp.where(lane < limit, turned[t], turned[t + 1])
            border_ref = first_ref.at[b] if b < AHEAD else second_ref.at[b - AHEAD]
            border_ref[:, t * LANES : (t + 1) * LANES] = tile.astype(jnp.bfloat16)
    for copy in copies[2 + bands * OWN :]:
        copy.wait()
    pack_into(blocks_ref, 0, obs, psf, rows)


def prep(sky, observed, psf, anchor, offsets, slots, distant):
    bands, rows_total = sky.shape[:2]
    per_device = observed.shape[1]
    hbm = pl.BlockSpec(memory_space=pltpu.HBM)
    vmem = pl.BlockSpec(memory_space=pltpu.VMEM)
    smem = pl.BlockSpec(memory_space=pltpu.SMEM)
    arrays = [pltpu.with_memory_space_constraint(x, pltpu.HBM) for x in (sky, observed, psf, anchor, offsets)]
    return pl.pallas_call(
        functools.partial(prep_kernel, distant),
        out_shape=(
            jax.ShapeDtypeStruct((bands, OWN, rows_total, LANES), jnp.bfloat16),
            jax.ShapeDtypeStruct((AHEAD, rows_total // FOLD, FOLDED * LANES), jnp.bfloat16),
            jax.ShapeDtypeStruct((bands - AHEAD, rows_total // FOLD, FOLDED * LANES), jnp.bfloat16),
            jax.ShapeDtypeStruct((per_device, bands, ROWS, LANES), jnp.bfloat16),
            jax.ShapeDtypeStruct((MODES, bands * slots + TOGETHER + 2), jnp.int32),
        ),
        in_specs=[hbm] * 5,
        out_specs=(vmem, vmem, vmem, vmem, smem),
        scratch_shapes=[
            pltpu.VMEM(observed.shape, jnp.bfloat16),
            pltpu.VMEM(psf.shape, jnp.bfloat16),
            pltpu.SMEM(anchor.shape, jnp.int32),
            pltpu.SMEM(offsets.shape, jnp.int32),
            pltpu.VMEM((8, bands * per_device, LANES), jnp.float32),
            pltpu.SemaphoreType.DMA((bands * OWN + 4,)),
        ],
        compiler_params=pltpu.CompilerParams(vmem_limit_bytes=SMALL_VMEM),
        cost_estimate=pl.CostEstimate(flops=0, bytes_accessed=1 << 20, transcendentals=0),
        name="prep",
    )(*arrays)


def merge_kernel(own_ref, obs_ref, psf_ref, both_ref, rows):
    both_ref[0:1] = own_ref[...]
    pack_into(both_ref, 1, obs_ref, psf_ref, rows)


def merge(own, observed, psf):
    vmem = pl.BlockSpec(memory_space=pltpu.VMEM)
    return pl.pallas_call(
        merge_kernel,
        out_shape=jax.ShapeDtypeStruct((2 * own.shape[0],) + own.shape[1:], jnp.bfloat16),
        in_specs=[vmem] * 3,
        out_specs=vmem,
        scratch_shapes=[pltpu.VMEM((8, psf.shape[0], LANES), jnp.float32)],
        compiler_params=pltpu.CompilerParams(vmem_limit_bytes=SMALL_VMEM),
        cost_estimate=pl.CostEstimate(flops=0, bytes_accessed=1 << 20, transcendentals=0),
        name="merge",
    )(own, observed, psf)


def list_windows(anchor_ref, offset_ref, plan_ref, bands, distant):
    column = lax.axis_index("sky")
    parity = column % 2
    first = column - parity
    slots = lax.axis_size("sky") * lax.axis_size("exp")
    position = column * lax.axis_size("exp") + lax.axis_index("exp")
    per_device = anchor_ref.shape[1] // slots
    cap = plan_ref.shape[1]
    begin = parity * TILE

    def code_of(b, n, top, start):
        code = jnp.int32(b << (FIELD[0] + FIELD[1] + FIELD[2]))
        return code + (n << (FIELD[0] + FIELD[1])) + (top << FIELD[1]) + start

    def visit(b, n, counts):
        near, inner, cross = counts
        known = jnp.int32(0)
        if distant:
            known = (jnp.bitwise_and(n - position, distant - 1) == 0).astype(jnp.int32)
        for x in range(per_device):
            i = n * per_device + x
            left = offset_ref[b, 1, i]
            here = anchor_ref[b, i] == first
            code = code_of(b, n, offset_ref[b, 0, i], left)
            if distant:
                plan_ref[0, near] = code - begin
            plan_ref[1, inner] = code - begin
            plan_ref[2, cross] = code - (TILE - LANES)
            start = left - begin
            inside = (here & (start >= 0) & (start <= TILE - WIN)).astype(jnp.int32)
            near = near + inside * known
            inner = inner + inside * (1 - known)
            cross = cross + (here & (left > TILE - WIN) & (left < TILE)).astype(jnp.int32)
        return near, inner, cross

    counts = (jnp.int32(0),) * MODES
    for b in range(bands):
        if slots <= 8:
            for n in range(slots):
                counts = visit(b, jnp.int32(n), counts)
        else:
            counts = lax.fori_loop(0, slots, functools.partial(visit, b), counts)
    for k in range(MODES):
        for extra in range(TOGETHER):
            plan_ref[k, counts[k] + extra] = code_of(bands - 1, jnp.int32(0), jnp.int32(0), jnp.int32(0))
        plan_ref[k, cap - 1] = counts[k]


def unfold(halo, border, b, place, rows_total):
    fold = rows_total // FOLD
    lane = jnp.bitwise_and(lane_of((fold, LANES)) - place, LANES - 1)
    tiles = [border[:, t * LANES : (t + 1) * LANES].astype(jnp.float32) for t in range(FOLDED)]
    for g in range(FOLD):
        shift = (place + LANES - WIN * g % LANES) % LANES
        first = WIN * g // LANES
        limit = LANES * (first + 1) - WIN * g
        value = pltpu.roll(tiles[first], shift, 1)
        if limit < WIN:
            value = jnp.where(lane < limit, value, pltpu.roll(tiles[first + 1], shift, 1))
        halo[b, g * fold : (g + 1) * fold, :] = value.astype(jnp.bfloat16)


def work_kernel(mode, resume, layout, plan_ref, sky_ref, *rest):
    late = mode == MODES - 1
    if late:
        first_ref, second_ref, *rest = rest
    if resume:
        sum_ref, *rest = rest
    pieces = rest[: len(layout)]
    rest = rest[len(layout) :]
    if late:
        out_hbm, total, halo, out_sems, *rest = rest
    else:
        total, *rest = rest
    blocks, cut0, cut1, view, banded0, banded1, wide0, wide1, rows_a, rows_r0, rows_r1 = rest
    cut, banded, wide, rows_r = (cut0, cut1), (banded0, banded1), (wide0, wide1), (rows_r0, rows_r1)
    bands, _, rows_total = sky_ref.shape[:3]
    column = lax.axis_index("sky")
    parity = column % 2
    position = column * lax.axis_size("exp") + lax.axis_index("exp")
    mine = list(range(bands))

    def out_copy(src, b, t, at):
        side = pl.multiple_of(t * LANES, LANES)
        return pltpu.make_async_copy(src, out_hbm.at[b, :, pl.ds(side, LANES)], out_sems.at[at])

    if late:
        finished = out_copies = [out_copy(sum_ref.at[b, parity], b, parity, b) for b in mine]
        for copy in finished:
            copy.start()
    for masks, piece in zip(layout, pieces):
        if masks is not None:
            for j, mask in enumerate(masks):
                blocks[jnp.bitwise_xor(position, mask)] = piece[j]
        else:
            blocks = piece
    count = plan_ref[mode, plan_ref.shape[1] - 1]
    for u in range(TOGETHER):
        rows_r[u][...] = jnp.zeros(rows_r[u].shape, jnp.float32)
        cut[u][CUT - 8 : CUT, :] = jnp.zeros((8, LANES), jnp.float32)
    for b in mine:
        if late:
            total[b, 0] = sum_ref[b, 1 - parity]
            border = first_ref[b] if b < AHEAD else second_ref[b - AHEAD]
            unfold(halo, border, b, parity * (LANES - WIN), rows_total)
        else:
            for t in range(OWN):
                total[b, t] = sum_ref[b, t] if resume else jnp.zeros((rows_total, LANES), jnp.float32)

    lane_w = lane_of((WPAD, LANES))
    gap = row_of((WPAD, LANES)) - lane_w % STAMP
    inside = (gap >= 0) & (gap < PSF) & (row_of((WPAD, LANES)) < WIN)
    lane_c = lane_of((CUT - 8, LANES))
    lane_b = lane_of((WIN, LANES))
    low = lane_of((STAMP, LANES)) < STAMP

    def where_is(job):
        code = plan_ref[mode, job]
        n = jnp.bitwise_and(lax.shift_right_logical(code, FIELD[0] + FIELD[1]), (1 << FIELD[2]) - 1)
        return lax.shift_right_logical(code, FIELD[0] + FIELD[1] + FIELD[2]), n, code

    def fields(job):
        b, n, code = where_is(job)
        top = jnp.bitwise_and(lax.shift_right_logical(code, FIELD[1]), (1 << FIELD[0]) - 1)
        start = jnp.bitwise_and(code, (1 << FIELD[1]) - 1)
        tile = lax.shift_right_logical(start, 7)
        shift = jnp.bitwise_and(start, LANES - 1)
        return b, n, top, tile, shift

    def load_window(job, u):
        b, _, top, tile, shift = fields(job)
        back_shift = jnp.bitwise_and(LANES - shift, LANES - 1)
        base = pl.multiple_of(jnp.minimum(jnp.bitwise_and(top, -16), rows_total - (CUT - 8)), 16)
        span = pl.ds(base, CUT - 8)
        if late:
            own = pltpu.roll(sky_ref[b, 1 - parity, span, :].astype(jnp.float32), back_shift, 1)
            other = pltpu.roll(halo[b, span, :].astype(jnp.float32), back_shift, 1)
            own_from = jnp.where(parity == 0, 0, LANES - shift)
            own_to = jnp.where(parity == 0, LANES - shift, LANES)
            window = jnp.where((lane_c >= own_from) & (lane_c < own_to), own, other)
        else:
            after = jnp.minimum(tile + 1, OWN - 1)
            left = pltpu.roll(sky_ref[b, tile, span, :].astype(jnp.float32), back_shift, 1)
            right = pltpu.roll(sky_ref[b, after, span, :].astype(jnp.float32), back_shift, 1)
            window = jnp.where(lane_c < LANES - shift, left, right)
        cut[u][0 : CUT - 8, :] = window
        view[u] = cut[u][pl.ds(top - base, WPAD), :].astype(jnp.bfloat16)

    def build(job, u, first, last):
        b, n, _ = where_is(job)
        taps = blocks[n, b, HALF:ROWS, :].astype(jnp.float32)
        for m in range(first, min(last, PAIRS)):
            row = m % SHARED
            spread = jnp.broadcast_to(taps[row : row + 1, :], (WPAD, LANES))
            offset = 0 if m < SHARED else LANES - ASIDE
            turned = pltpu.roll(spread, offset, 1, stride=1, stride_axis=0)
            banded[u][:, m * LANES : (m + 1) * LANES] = jnp.where(inside, turned, 0.0).astype(jnp.bfloat16)

    def forward(u, first, last):
        last = min(last, PAIRS)
        product = jnp.dot(
            view[u, :, :WPAD],
            banded[u][:, first * LANES : last * LANES],
            preferred_element_type=jnp.float32,
        )
        for m in range(first, last):
            wide[u][m] = product[:, (m - first) * LANES : (m - first + 1) * LANES]

    def residual(job, u):
        b, n, _ = where_is(job)
        acc = wide[u][0, 0:72, :]
        for m in range(1, PAIRS):
            acc = acc + wide[u][m, 2 * m : 2 * m + 72, :]
        rows_a[u] = acc
        model = rows_a[u, 0:STAMP, :] + pltpu.roll(rows_a[u, 1 : STAMP + 1, :], STAMP, 1)
        obs = blocks[n, b, 0:HALF, :].astype(jnp.float32)
        obs = jnp.concatenate([obs, pltpu.roll(obs, STAMP, 1)], axis=0)
        rest = (model - obs).astype(jnp.bfloat16).astype(jnp.float32)
        rest = jnp.where(low, rest, 0.0)
        rows_r[u][EDGE : EDGE + STAMP, :] = rest
        rows_r[u][EDGE + STAMP : EDGE + 72, :] = jnp.zeros((8, LANES), jnp.float32)
        upper = pltpu.roll(rows_r[u][EDGE - 1 : EDGE + 71, :], STAMP, 1)
        rows_r[u][EDGE : EDGE + 72, :] = rows_r[u][EDGE : EDGE + 72, :] + upper

    def backward(u):
        stack = [
            rows_r[u][EDGE - 2 * m : EDGE - 2 * m + WIN, :].astype(jnp.bfloat16) for m in range(PAIRS)
        ]
        back = lax.dot_general(
            jnp.concatenate(stack, axis=1),
            banded[u][...],
            (((1,), (1,)), ((), ())),
            preferred_element_type=jnp.float32,
        )
        back = back.astype(jnp.bfloat16).astype(jnp.float32)
        return jnp.concatenate([back, jnp.zeros((WIN, LANES - WPAD), jnp.float32)], axis=1)

    def add(job, back):
        b, _, top, tile, shift = fields(job)
        back = pltpu.roll(back, shift, 1)
        live = job < count
        begin = jnp.where(live, shift, LANES)
        end = jnp.where(live, shift, 0)
        here = pl.ds(top, WIN)
        if late:
            own_from = jnp.where(parity == 0, begin, 0)
            own_to = jnp.where(parity == 0, LANES, end)
            total[b, 0, here, :] += jnp.where((lane_b >= own_from) & (lane_b < own_to), back, 0.0)
        else:
            after = jnp.minimum(tile + 1, OWN - 1)
            total[b, tile, here, :] += jnp.where(lane_b >= begin, back, 0.0)
            total[b, after, here, :] += jnp.where(lane_b < end, back, 0.0)

    if late:
        closing = [out_copy(total.at[b, 0], b, 1 - parity, bands + b) for b in mine]
        out_copies = finished + closing

    def flush(b, ready):
        if late:

            @pl.when(ready)
            def _():
                closing[b].start()

    def step(index, before):
        one = index * 2
        two = one + 1
        now = where_is(one)[0]
        for b in mine[:-1]:
            flush(b, (before <= b) & (now > b))
        load_window(two, 1)
        for c in range(0, PAIRS, 2):
            forward(0, c, c + 2)
            build(two, 1, c, c + 2)
        residual(one, 0)
        for c in range(0, PAIRS, 2):
            forward(1, c, c + 2)
        back_one = backward(0)
        residual(two, 1)
        back_two = backward(1)
        add(one, back_one)
        load_window(one + 2, 0)
        build(one + 2, 0, 0, PAIRS)
        add(two, back_two)
        return now

    load_window(0, 0)
    build(0, 0, 0, PAIRS)
    before = lax.fori_loop(0, lax.div(count + 1, 2), step, jnp.int32(0))
    for b in mine:
        flush(b, before <= b)
    if late:
        for copy in out_copies:
            copy.wait()


def work(mode, plan, sky, pieces, layout, slots, so_far=None, borders=()):
    late = mode == MODES - 1
    bands, _, rows_total = sky.shape[:3]
    smem = pl.BlockSpec(memory_space=pltpu.SMEM)
    hbm = pl.BlockSpec(memory_space=pltpu.HBM)
    vmem = pl.BlockSpec(memory_space=pltpu.VMEM)
    gathered = (slots, bands, ROWS, LANES) if layout[0] is not None else (1, 1, 8, LANES)
    first = list(borders) + ([] if so_far is None else [so_far])
    if late:
        out_shape = jax.ShapeDtypeStruct((bands, rows_total, TILE), jnp.float32)
        own_scratch = [
            pltpu.VMEM((bands, 1, rows_total, LANES), jnp.float32),
            pltpu.VMEM((bands, rows_total, LANES), jnp.bfloat16),
            pltpu.SemaphoreType.DMA((2 * bands,)),
        ]
    else:
        out_shape = jax.ShapeDtypeStruct((bands, OWN, rows_total, LANES), jnp.float32)
        own_scratch = []
    return pl.pallas_call(
        functools.partial(work_kernel, mode, so_far is not None, layout),
        out_shape=out_shape,
        in_specs=[smem, vmem] + [vmem] * (len(first) + len(pieces)),
        out_specs=hbm if late else vmem,
        scratch_shapes=own_scratch
        + [pltpu.VMEM(gathered, jnp.bfloat16)]
        + [pltpu.VMEM((CUT, LANES), jnp.float32)] * 2
        + [pltpu.VMEM((TOGETHER, WPAD, LANES), jnp.bfloat16)]
        + [pltpu.VMEM((WPAD, PAIRS * LANES), jnp.bfloat16)] * 2
        + [pltpu.VMEM((PAIRS, WPAD, LANES), jnp.float32)] * 2
        + [pltpu.VMEM((TOGETHER, 72, LANES), jnp.float32)]
        + [pltpu.VMEM((112, LANES), jnp.float32)] * 2,
        compiler_params=pltpu.CompilerParams(vmem_limit_bytes=WORK_VMEM),
        cost_estimate=pl.CostEstimate(flops=0, bytes_accessed=8 << 20, transcendentals=0),
    )(plan, sky, *first, *pieces)


def on_device(sky, observed, psf, anchor, offsets):
    bands = sky.shape[0]
    per_device = observed.shape[1]
    n_sky = lax.axis_size("sky")
    n_exp = lax.axis_size("exp")
    slots = n_sky * n_exp
    both = ("sky", "exp")
    taps = psf.reshape(bands * per_device, psf.shape[-1])
    direct = per_device == 1 and n_sky == 4 and n_exp == 2

    def across(x, mask):
        return lax.ppermute(x, both, [(i, i ^ mask) for i in range(slots)])

    def neighbour(x):
        return lax.ppermute(x, "sky", [(s, s ^ 1) for s in range(n_sky)])

    if direct:
        far_observed = across(observed, 4)
        far_taps = across(taps, 4)
    tiles, ahead, border, blocks, plan = prep(sky, observed, taps, anchor, offsets, slots, slots // 2 if direct else 0)
    halo_ahead = neighbour(ahead)
    if direct:
        own = merge(blocks, far_observed, far_taps)
        pieces = [own]
        layout = [(0, 4)]
        for mask in (3, 2, 1):
            pieces.append(across(own, mask))
            layout.append((mask, mask ^ 4))
    else:
        position = lax.axis_index("sky") * n_exp + lax.axis_index("exp")
        anchors = anchor.reshape(bands, slots, per_device)
        mine = lax.dynamic_index_in_dim(anchors, position, 1, keepdims=False)
        pair = 2 * jnp.arange(n_sky // 2, dtype=jnp.int32)[:, None, None]
        chosen = jnp.argmax(mine[None] == pair, axis=-1)
        picked = jnp.take_along_axis(blocks[None], chosen[:, None, :, None, None], axis=1)
        send = jnp.broadcast_to(picked, (n_sky // 2, 2 * n_exp, bands, ROWS, LANES))
        send = send.reshape(slots, bands, ROWS, LANES)
        pieces = [lax.all_to_all(send, both, 0, 0, tiled=True)]
        layout = [None]
    halo = neighbour(border)
    so_far, done = None, 0
    if direct:
        so_far, done = work(0, plan, tiles, pieces[:1], layout[:1], slots), 1
    so_far = work(1, plan, tiles, pieces[done:], layout[done:], slots, so_far)
    return work(2, plan, tiles, pieces, layout, slots, so_far, (halo_ahead, halo))


def solution(mesh):
    return jax.shard_map(
        on_device,
        mesh=mesh,
        in_specs=(
            P("band", None, ("group", "sky")),
            P("band", ("group", "sky", "exp"), None, None),
            P("band", ("group", "sky", "exp"), None),
            P("band", "group"),
            P("band", None, "group"),
        ),
        out_specs=P("band", None, ("group", "sky")),
        check_vma=False,
    )
```

```python
import functools

import jax
import jax.numpy as jnp
from jax import lax
from jax.experimental import pallas as pl
from jax.experimental.pallas import tpu as pltpu
from jax.sharding import PartitionSpec as P

TILE = 256
PSF = 25
STAMP = 64
HALF = STAMP // 2
WIN = 88
LANES = 128
PAIRS = (PSF + 1) // 2
ROWS = 40
SHARED = 7
ASIDE = 32
WPAD = 96
OWN = TILE // LANES
FOLDED = 3
EDGE = PSF - 1
FOLD = 4
TOGETHER = 2
MODES = 3
AHEAD = 1
FIELD = (9, 9, 7)
SMALL_VMEM = 8 << 20
WORK_VMEM = 24 << 20
CUT = 120


def lane_of(shape):
    return lax.broadcasted_iota(jnp.int32, shape, 1)


def row_of(shape):
    return lax.broadcasted_iota(jnp.int32, shape, 0)


def pack_into(blocks_ref, at, obs_ref, psf_ref, rows):
    bands, per_device = obs_ref.shape[:2]
    lines = bands * per_device
    taps = PSF * PSF
    lane = lane_of((lines, LANES))
    turn = (lane_of((LANES, LANES)) + row_of((LANES, LANES))) == LANES - 1
    turn = jnp.where(turn, 1.0, 0.0).astype(jnp.bfloat16)
    tiles = []
    for t in range(pl.cdiv(taps, LANES)):
        tile = psf_ref[:, t * LANES : min((t + 1) * LANES, taps)]
        if tile.shape[1] < LANES:
            tile = jnp.concatenate([tile, jnp.zeros((lines, LANES - tile.shape[1]), tile.dtype)], axis=1)
        tiles.append(jnp.dot(tile, turn, preferred_element_type=jnp.float32))

    def run(first, target, count=PSF):
        t, end = first // LANES, (first + count - 1) // LANES
        value = tiles[t] if end == t else jnp.where(lane < LANES // 2, tiles[t], tiles[end])
        value = pltpu.roll(value, (target + first + 1) % LANES, 1)
        return jnp.where(jnp.bitwise_and(target - lane, LANES - 1) < count, value, 0.0)

    for r in range(8):
        row = jnp.zeros((lines, LANES), jnp.float32)
        for m, aside in ((r, 0), (r + SHARED, ASIDE)):
            if r < SHARED and m < PAIRS:
                row = row + run(2 * PSF * m, aside)
                if 2 * m + 1 < PSF:
                    row = row + run(2 * PSF * m + PSF, aside + STAMP)
        rows[r] = row
    for x in range(per_device):
        for b in range(bands):
            stamp = obs_ref[b, x].astype(jnp.float32)
            both = jnp.concatenate([stamp[:HALF], stamp[HALF:]], axis=1)
            blocks_ref[at + x, b, 0:HALF, :] = both.astype(jnp.bfloat16)
            blocks_ref[at + x, b, HALF:ROWS, :] = rows[:, b * per_device + x, :].astype(jnp.bfloat16)


def prep_kernel(
    distant, sky_hbm, obs_hbm, psf_hbm, anchor_hbm, offset_hbm,
    sky_ref, first_ref, second_ref, blocks_ref, plan_ref,
    obs, psf, anchor, offset, rows, sems,
):
    bands, rows_total = sky_hbm.shape[:2]
    parity = lax.axis_index("sky") % 2
    copies = []

    def bring(src, dst):
        copies.append(pltpu.make_async_copy(src, dst, sems.at[len(copies)]))

    bring(anchor_hbm, anchor)
    bring(offset_hbm, offset)
    for b in range(bands):
        for t in range(OWN):
            bring(sky_hbm.at[b, :, pl.ds(t * LANES, LANES)], sky_ref.at[b, t])
    bring(psf_hbm, psf)
    bring(obs_hbm, obs)
    for copy in copies:
        copy.start()
    copies[0].wait()
    copies[1].wait()
    list_windows(anchor, offset, plan_ref, bands, distant)
    fold = rows_total // FOLD
    lane = lane_of((fold, LANES))
    base = (1 - parity) * WIN
    for b in range(bands):
        for t in range(OWN):
            copies[2 + b * OWN + t].wait()
        turned = []
        for g in range(FOLD):
            part = sky_ref[b, 1 - parity, g * fold : (g + 1) * fold, :].astype(jnp.float32)
            turned.append(pltpu.roll(part, (base + WIN * g) % LANES, 1))
        for t in range(FOLDED):
            limit = WIN * (t + 1) - LANES * t
            tile = jnp.where(lane < limit, turned[t], turned[t + 1])
            border_ref = first_ref.at[b] if b < AHEAD else second_ref.at[b - AHEAD]
            border_ref[:, t * LANES : (t + 1) * LANES] = tile.astype(jnp.bfloat16)
    for copy in copies[2 + bands * OWN :]:
        copy.wait()
    pack_into(blocks_ref, 0, obs, psf, rows)


def prep(sky, observed, psf, anchor, offsets, slots, distant):
    bands, rows_total = sky.shape[:2]
    per_device = observed.shape[1]
    hbm = pl.BlockSpec(memory_space=pltpu.HBM)
    vmem = pl.BlockSpec(memory_space=pltpu.VMEM)
    smem = pl.BlockSpec(memory_space=pltpu.SMEM)
    arrays = [pltpu.with_memory_space_constraint(x, pltpu.HBM) for x in (sky, observed, psf, anchor, offsets)]
    return pl.pallas_call(
        functools.partial(prep_kernel, distant),
        out_shape=(
            jax.ShapeDtypeStruct((bands, OWN, rows_total, LANES), jnp.bfloat16),
            jax.ShapeDtypeStruct((AHEAD, rows_total // FOLD, FOLDED * LANES), jnp.bfloat16),
            jax.ShapeDtypeStruct((bands - AHEAD, rows_total // FOLD, FOLDED * LANES), jnp.bfloat16),
            jax.ShapeDtypeStruct((per_device, bands, ROWS, LANES), jnp.bfloat16),
            jax.ShapeDtypeStruct((MODES, bands * slots + TOGETHER + 2), jnp.int32),
        ),
        in_specs=[hbm] * 5,
        out_specs=(vmem, vmem, vmem, vmem, smem),
        scratch_shapes=[
            pltpu.VMEM(observed.shape, jnp.bfloat16),
            pltpu.VMEM(psf.shape, jnp.bfloat16),
            pltpu.SMEM(anchor.shape, jnp.int32),
            pltpu.SMEM(offsets.shape, jnp.int32),
            pltpu.VMEM((8, bands * per_device, LANES), jnp.float32),
            pltpu.SemaphoreType.DMA((bands * OWN + 4,)),
        ],
        compiler_params=pltpu.CompilerParams(vmem_limit_bytes=SMALL_VMEM),
        cost_estimate=pl.CostEstimate(flops=0, bytes_accessed=1 << 20, transcendentals=0),
        name="prep",
    )(*arrays)


def merge_kernel(own_ref, far_ref, both_ref):
    both_ref[0:1] = own_ref[...]
    both_ref[1:2] = far_ref[...]


def merge(own, far):
    vmem = pl.BlockSpec(memory_space=pltpu.VMEM)
    return pl.pallas_call(
        merge_kernel,
        out_shape=jax.ShapeDtypeStruct((2 * own.shape[0],) + own.shape[1:], jnp.bfloat16),
        in_specs=[vmem] * 2,
        out_specs=vmem,
        compiler_params=pltpu.CompilerParams(vmem_limit_bytes=SMALL_VMEM),
        cost_estimate=pl.CostEstimate(flops=0, bytes_accessed=1 << 20, transcendentals=0),
        name="merge",
    )(own, far)


def list_windows(anchor_ref, offset_ref, plan_ref, bands, distant):
    column = lax.axis_index("sky")
    parity = column % 2
    first = column - parity
    slots = lax.axis_size("sky") * lax.axis_size("exp")
    position = column * lax.axis_size("exp") + lax.axis_index("exp")
    per_device = anchor_ref.shape[1] // slots
    cap = plan_ref.shape[1]
    begin = parity * TILE

    def code_of(b, n, top, start):
        code = jnp.int32(b << (FIELD[0] + FIELD[1] + FIELD[2]))
        return code + (n << (FIELD[0] + FIELD[1])) + (top << FIELD[1]) + start

    def visit(b, n, counts):
        near, inner, cross = counts
        known = jnp.int32(0)
        if distant:
            known = (jnp.bitwise_and(n - position, distant - 1) == 0).astype(jnp.int32)
        for x in range(per_device):
            i = n * per_device + x
            left = offset_ref[b, 1, i]
            here = anchor_ref[b, i] == first
            code = code_of(b, n, offset_ref[b, 0, i], left)
            if distant:
                plan_ref[0, near] = code - begin
            plan_ref[1, inner] = code - begin
            plan_ref[2, cross] = code - (TILE - LANES)
            start = left - begin
            inside = (here & (start >= 0) & (start <= TILE - WIN)).astype(jnp.int32)
            near = near + inside * known
            inner = inner + inside * (1 - known)
            cross = cross + (here & (left > TILE - WIN) & (left < TILE)).astype(jnp.int32)
        return near, inner, cross

    counts = (jnp.int32(0),) * MODES
    for b in range(bands):
        if slots <= 8:
            for n in range(slots):
                counts = visit(b, jnp.int32(n), counts)
        else:
            counts = lax.fori_loop(0, slots, functools.partial(visit, b), counts)
    for k in range(MODES):
        for extra in range(TOGETHER):
            plan_ref[k, counts[k] + extra] = code_of(bands - 1, jnp.int32(0), jnp.int32(0), jnp.int32(0))
        plan_ref[k, cap - 1] = counts[k]


def unfold(halo, border, b, place, rows_total):
    fold = rows_total // FOLD
    lane = jnp.bitwise_and(lane_of((fold, LANES)) - place, LANES - 1)
    tiles = [border[:, t * LANES : (t + 1) * LANES].astype(jnp.float32) for t in range(FOLDED)]
    for g in range(FOLD):
        shift = (place + LANES - WIN * g % LANES) % LANES
        first = WIN * g // LANES
        limit = LANES * (first + 1) - WIN * g
        value = pltpu.roll(tiles[first], shift, 1)
        if limit < WIN:
            value = jnp.where(lane < limit, value, pltpu.roll(tiles[first + 1], shift, 1))
        halo[b, g * fold : (g + 1) * fold, :] = value.astype(jnp.bfloat16)


def work_kernel(mode, resume, layout, plan_ref, sky_ref, *rest):
    late = mode == MODES - 1
    if late:
        first_ref, second_ref, *rest = rest
    if resume:
        sum_ref, *rest = rest
    pieces = rest[: len(layout)]
    rest = rest[len(layout) :]
    if late:
        out_hbm, total, halo, out_sems, *rest = rest
    else:
        total, *rest = rest
    blocks, cut0, cut1, view, banded0, banded1, wide0, wide1, rows_a, rows_r0, rows_r1 = rest
    cut, banded, wide, rows_r = (cut0, cut1), (banded0, banded1), (wide0, wide1), (rows_r0, rows_r1)
    bands, _, rows_total = sky_ref.shape[:3]
    column = lax.axis_index("sky")
    parity = column % 2
    position = column * lax.axis_size("exp") + lax.axis_index("exp")
    mine = list(range(bands))

    def out_copy(src, b, t, at):
        side = pl.multiple_of(t * LANES, LANES)
        return pltpu.make_async_copy(src, out_hbm.at[b, :, pl.ds(side, LANES)], out_sems.at[at])

    if late:
        finished = out_copies = [out_copy(sum_ref.at[b, parity], b, parity, b) for b in mine]
        for copy in finished:
            copy.start()
    for masks, piece in zip(layout, pieces):
        if masks is not None:
            for j, mask in enumerate(masks):
                blocks[jnp.bitwise_xor(position, mask)] = piece[j]
        else:
            blocks = piece
    count = plan_ref[mode, plan_ref.shape[1] - 1]
    for u in range(TOGETHER):
        rows_r[u][...] = jnp.zeros(rows_r[u].shape, jnp.float32)
        cut[u][CUT - 8 : CUT, :] = jnp.zeros((8, LANES), jnp.float32)
    for b in mine:
        if late:
            total[b, 0] = sum_ref[b, 1 - parity]
            border = first_ref[b] if b < AHEAD else second_ref[b - AHEAD]
            unfold(halo, border, b, parity * (LANES - WIN), rows_total)
        else:
            for t in range(OWN):
                total[b, t] = sum_ref[b, t] if resume else jnp.zeros((rows_total, LANES), jnp.float32)

    lane_w = lane_of((WPAD, LANES))
    gap = row_of((WPAD, LANES)) - lane_w % STAMP
    inside = (gap >= 0) & (gap < PSF) & (row_of((WPAD, LANES)) < WIN)
    lane_c = lane_of((CUT - 8, LANES))
    lane_b = lane_of((WIN, LANES))
    low = lane_of((STAMP, LANES)) < STAMP

    def where_is(job):
        code = plan_ref[mode, job]
        n = jnp.bitwise_and(lax.shift_right_logical(code, FIELD[0] + FIELD[1]), (1 << FIELD[2]) - 1)
        return lax.shift_right_logical(code, FIELD[0] + FIELD[1] + FIELD[2]), n, code

    def fields(job):
        b, n, code = where_is(job)
        top = jnp.bitwise_and(lax.shift_right_logical(code, FIELD[1]), (1 << FIELD[0]) - 1)
        start = jnp.bitwise_and(code, (1 << FIELD[1]) - 1)
        tile = lax.shift_right_logical(start, 7)
        shift = jnp.bitwise_and(start, LANES - 1)
        return b, n, top, tile, shift

    def load_window(job, u):
        b, _, top, tile, shift = fields(job)
        back_shift = jnp.bitwise_and(LANES - shift, LANES - 1)
        base = pl.multiple_of(jnp.minimum(jnp.bitwise_and(top, -16), rows_total - (CUT - 8)), 16)
        span = pl.ds(base, CUT - 8)
        if late:
            own = pltpu.roll(sky_ref[b, 1 - parity, span, :].astype(jnp.float32), back_shift, 1)
            other = pltpu.roll(halo[b, span, :].astype(jnp.float32), back_shift, 1)
            own_from = jnp.where(parity == 0, 0, LANES - shift)
            own_to = jnp.where(parity == 0, LANES - shift, LANES)
            window = jnp.where((lane_c >= own_from) & (lane_c < own_to), own, other)
        else:
            after = jnp.minimum(tile + 1, OWN - 1)
            left = pltpu.roll(sky_ref[b, tile, span, :].astype(jnp.float32), back_shift, 1)
            right = pltpu.roll(sky_ref[b, after, span, :].astype(jnp.float32), back_shift, 1)
            window = jnp.where(lane_c < LANES - shift, left, right)
        cut[u][0 : CUT - 8, :] = window
        view[u] = cut[u][pl.ds(top - base, WPAD), :].astype(jnp.bfloat16)

    def build(job, u, first, last):
        b, n, _ = where_is(job)
        taps = blocks[n, b, HALF:ROWS, :].astype(jnp.float32)
        for m in range(first, min(last, PAIRS)):
            row = m % SHARED
            spread = jnp.broadcast_to(taps[row : row + 1, :], (WPAD, LANES))
            offset = 0 if m < SHARED else LANES - ASIDE
            turned = pltpu.roll(spread, offset, 1, stride=1, stride_axis=0)
            banded[u][:, m * LANES : (m + 1) * LANES] = jnp.where(inside, turned, 0.0).astype(jnp.bfloat16)

    def forward(u, first, last):
        last = min(last, PAIRS)
        product = jnp.dot(
            view[u, :, :WPAD],
            banded[u][:, first * LANES : last * LANES],
            preferred_element_type=jnp.float32,
        )
        for m in range(first, last):
            wide[u][m] = product[:, (m - first) * LANES : (m - first + 1) * LANES]

    def residual(job, u):
        b, n, _ = where_is(job)
        acc = wide[u][0, 0:72, :]
        for m in range(1, PAIRS):
            acc = acc + wide[u][m, 2 * m : 2 * m + 72, :]
        rows_a[u] = acc
        model = rows_a[u, 0:STAMP, :] + pltpu.roll(rows_a[u, 1 : STAMP + 1, :], STAMP, 1)
        obs = blocks[n, b, 0:HALF, :].astype(jnp.float32)
        obs = jnp.concatenate([obs, pltpu.roll(obs, STAMP, 1)], axis=0)
        rest = (model - obs).astype(jnp.bfloat16).astype(jnp.float32)
        rest = jnp.where(low, rest, 0.0)
        rows_r[u][EDGE : EDGE + STAMP, :] = rest
        rows_r[u][EDGE + STAMP : EDGE + 72, :] = jnp.zeros((8, LANES), jnp.float32)
        upper = pltpu.roll(rows_r[u][EDGE - 1 : EDGE + 71, :], STAMP, 1)
        rows_r[u][EDGE : EDGE + 72, :] = rows_r[u][EDGE : EDGE + 72, :] + upper

    def backward(u):
        stack = [
            rows_r[u][EDGE - 2 * m : EDGE - 2 * m + WIN, :].astype(jnp.bfloat16) for m in range(PAIRS)
        ]
        back = lax.dot_general(
            jnp.concatenate(stack, axis=1),
            banded[u][...],
            (((1,), (1,)), ((), ())),
            preferred_element_type=jnp.float32,
        )
        back = back.astype(jnp.bfloat16).astype(jnp.float32)
        return jnp.concatenate([back, jnp.zeros((WIN, LANES - WPAD), jnp.float32)], axis=1)

    def add(job, back):
        b, _, top, tile, shift = fields(job)
        back = pltpu.roll(back, shift, 1)
        live = job < count
        begin = jnp.where(live, shift, LANES)
        end = jnp.where(live, shift, 0)
        here = pl.ds(top, WIN)
        if late:
            own_from = jnp.where(parity == 0, begin, 0)
            own_to = jnp.where(parity == 0, LANES, end)
            total[b, 0, here, :] += jnp.where((lane_b >= own_from) & (lane_b < own_to), back, 0.0)
        else:
            after = jnp.minimum(tile + 1, OWN - 1)
            total[b, tile, here, :] += jnp.where(lane_b >= begin, back, 0.0)
            total[b, after, here, :] += jnp.where(lane_b < end, back, 0.0)

    if late:
        closing = [out_copy(total.at[b, 0], b, 1 - parity, bands + b) for b in mine]
        out_copies = finished + closing

    def flush(b, ready):
        if late:

            @pl.when(ready)
            def _():
                closing[b].start()

    def step(index, before):
        one = index * 2
        two = one + 1
        now = where_is(one)[0]
        for b in mine[:-1]:
            flush(b, (before <= b) & (now > b))
        load_window(two, 1)
        for c in range(0, PAIRS, 2):
            forward(0, c, c + 2)
            build(two, 1, c, c + 2)
        residual(one, 0)
        for c in range(0, PAIRS, 2):
            forward(1, c, c + 2)
        back_one = backward(0)
        residual(two, 1)
        back_two = backward(1)
        add(one, back_one)
        load_window(one + 2, 0)
        build(one + 2, 0, 0, PAIRS)
        add(two, back_two)
        return now

    load_window(0, 0)
    build(0, 0, 0, PAIRS)
    before = lax.fori_loop(0, lax.div(count + 1, 2), step, jnp.int32(0))
    for b in mine:
        flush(b, before <= b)
    if late:
        for copy in out_copies:
            copy.wait()


def work(mode, plan, sky, pieces, layout, slots, so_far=None, borders=()):
    late = mode == MODES - 1
    bands, _, rows_total = sky.shape[:3]
    smem = pl.BlockSpec(memory_space=pltpu.SMEM)
    hbm = pl.BlockSpec(memory_space=pltpu.HBM)
    vmem = pl.BlockSpec(memory_space=pltpu.VMEM)
    gathered = (slots, bands, ROWS, LANES) if layout[0] is not None else (1, 1, 8, LANES)
    first = list(borders) + ([] if so_far is None else [so_far])
    if late:
        out_shape = jax.ShapeDtypeStruct((bands, rows_total, TILE), jnp.float32)
        own_scratch = [
            pltpu.VMEM((bands, 1, rows_total, LANES), jnp.float32),
            pltpu.VMEM((bands, rows_total, LANES), jnp.bfloat16),
            pltpu.SemaphoreType.DMA((2 * bands,)),
        ]
    else:
        out_shape = jax.ShapeDtypeStruct((bands, OWN, rows_total, LANES), jnp.float32)
        own_scratch = []
    return pl.pallas_call(
        functools.partial(work_kernel, mode, so_far is not None, layout),
        out_shape=out_shape,
        in_specs=[smem, vmem] + [vmem] * (len(first) + len(pieces)),
        out_specs=hbm if late else vmem,
        scratch_shapes=own_scratch
        + [pltpu.VMEM(gathered, jnp.bfloat16)]
        + [pltpu.VMEM((CUT, LANES), jnp.float32)] * 2
        + [pltpu.VMEM((TOGETHER, WPAD, LANES), jnp.bfloat16)]
        + [pltpu.VMEM((WPAD, PAIRS * LANES), jnp.bfloat16)] * 2
        + [pltpu.VMEM((PAIRS, WPAD, LANES), jnp.float32)] * 2
        + [pltpu.VMEM((TOGETHER, 72, LANES), jnp.float32)]
        + [pltpu.VMEM((112, LANES), jnp.float32)] * 2,
        compiler_params=pltpu.CompilerParams(vmem_limit_bytes=WORK_VMEM),
        cost_estimate=pl.CostEstimate(flops=0, bytes_accessed=8 << 20, transcendentals=0),
    )(plan, sky, *first, *pieces)


def on_device(sky, observed, psf, anchor, offsets):
    bands = sky.shape[0]
    per_device = observed.shape[1]
    n_sky = lax.axis_size("sky")
    n_exp = lax.axis_size("exp")
    slots = n_sky * n_exp
    both = ("sky", "exp")
    taps = psf.reshape(bands * per_device, psf.shape[-1])
    direct = per_device == 1 and n_sky == 4 and n_exp == 2

    def across(x, mask):
        return lax.ppermute(x, both, [(i, i ^ mask) for i in range(slots)])

    def neighbour(x):
        return lax.ppermute(x, "sky", [(s, s ^ 1) for s in range(n_sky)])

    tiles, ahead, border, blocks, plan = prep(sky, observed, taps, anchor, offsets, slots, slots // 2 if direct else 0)
    if direct:
        far = across(blocks, slots // 2)
    halo_ahead = neighbour(ahead)
    if direct:
        own = merge(blocks, far)
        pieces = [own]
        layout = [(0, 4)]
        for mask in (3, 2, 1):
            pieces.append(across(own, mask))
            layout.append((mask, mask ^ 4))
    else:
        position = lax.axis_index("sky") * n_exp + lax.axis_index("exp")
        anchors = anchor.reshape(bands, slots, per_device)
        mine = lax.dynamic_index_in_dim(anchors, position, 1, keepdims=False)
        pair = 2 * jnp.arange(n_sky // 2, dtype=jnp.int32)[:, None, None]
        chosen = jnp.argmax(mine[None] == pair, axis=-1)
        picked = jnp.take_along_axis(blocks[None], chosen[:, None, :, None, None], axis=1)
        send = jnp.broadcast_to(picked, (n_sky // 2, 2 * n_exp, bands, ROWS, LANES))
        send = send.reshape(slots, bands, ROWS, LANES)
        pieces = [lax.all_to_all(send, both, 0, 0, tiled=True)]
        layout = [None]
    halo = neighbour(border)
    so_far, done = None, 0
    if direct:
        so_far, done = work(0, plan, tiles, pieces[:1], layout[:1], slots), 1
    so_far = work(1, plan, tiles, pieces[done:], layout[done:], slots, so_far)
    return work(2, plan, tiles, pieces, layout, slots, so_far, (halo_ahead, halo))


def solution(mesh):
    return jax.shard_map(
        on_device,
        mesh=mesh,
        in_specs=(
            P("band", None, ("group", "sky")),
            P("band", ("group", "sky", "exp"), None, None),
            P("band", ("group", "sky", "exp"), None),
            P("band", "group"),
            P("band", None, "group"),
        ),
        out_specs=P("band", None, ("group", "sky")),
        check_vma=False,
    )
```
